256 devices in a mesh: tok: 32 (over z, y_hi, core), row: 2 (over y_lo), col: 4 (over x).
Axes of the slice: x: 4, y: 4 (y_hi: 2, y_lo: 2; y = y_hi * 2 + y_lo), z: 8, core: 2. Of those that a mesh axis runs over, the one named last changes fastest.
Arguments:
- activations: bfloat16 [11264, 4096], P(('tok', 'row'), 'col'), may hold values from -512 to 512
- norm_gain: bfloat16 [4096], P('col'), may hold values from 1.5 to 10
- qkv_weight: bfloat16 [4096, 16, 384], P('row', 'col'), may hold values from -0.09375 to 0.09375
- doc_ids: int32 [11264], P(('tok', 'row')), may hold values from 0 to 3, never falling along the last dimension, each value on 1 to 8448 neighbouring positions
Outputs:
- attended: bfloat16 [11264, 2048], P(('tok', 'row'), 'col')
The draws below stay inside these ranges and needn't reach their ends.
Inputs may be any that keep to these rules, and one draw needn't show every extreme that they name: `doc_ids`: never falls along the sequence; each of the 4 documents holds 1 to 8448 tokens and one holds exactly 8448.
All inputs are finite; a program needn't handle non-finite values.
Results may differ from the reference program's by a relative error of at most 0.007.
The reference program's roundings to bfloat16 on the way (of `normed`, `query`, `keys`, `values` and `weights`) count: a program that leaves them out, or rounds other values in their place, can miss the bound.
Values may be sent and summed in bfloat16 or wider, within the bound.
A program may use at most 128 MiB of HBM per device.

```python
import math
import jax
import jax.numpy as jnp
import numpy as np
from jax import lax

D = 4096
HEADS = 16
HEAD_DIM = 128
DOCS = 4
TOKENS = 11264
DOC_MOST = 8448


def draw_activations(key, part):
    column_key, row_key, base_key = jax.random.split(key, 3)
    column_scale = jnp.exp(jax.random.uniform(column_key, (1, D), jnp.float32, 0.0, math.log(10.0)))
    row_scale = jnp.exp(jax.random.uniform(row_key, (TOKENS, 1), jnp.float32, 0.0, math.log(10.0)))
    values = jax.random.normal(base_key, (TOKENS, D), jnp.float32) * column_scale * row_scale
    return jnp.clip(values, -512.0, 512.0).astype(jnp.bfloat16)


def draw_norm_gain(key, part):
    lowest = 1.5
    highest = 6.0
    drawn = jax.random.uniform(key, (D,), jnp.float32, math.log(lowest), math.log(highest))
    return jnp.exp(drawn).astype(jnp.bfloat16)


def level_of(stream_key, dims, cuts, smallest, largest):
    def one(position, shards_of):
        heights = jax.random.uniform(jax.random.fold_in(jax.random.fold_in(stream_key, 6), position), (shards_of,), jnp.float32, smallest / len(cuts), largest / len(cuts))
        return jnp.repeat(jnp.exp(heights), dims[position] // shards_of).reshape((-1,) + (1,) * (len(dims) - position - 1))

    factor_of = one(*cuts[0])
    for cut in cuts[1:]:
        factor_of = factor_of * one(*cut)
    return factor_of


def length_profile(count, total, bound, skew):
    weights = [(1 << 20) // math.isqrt(standing ** skew) + 1 for standing in range(2, count + 1)]
    rest, counts = total - bound - (count - 1), [1] * (count - 1)
    while rest > 0:
        candidates = [i for i in range(count - 1) if counts[i] < bound]
        mass, remaining = sum([weights[i] for i in candidates]), rest
        for i in candidates:
            addition = min(bound - counts[i], max(1, remaining * weights[i] // mass), rest)
            counts[i] = counts[i] + addition
            rest = rest - addition
    return np.array([bound] + counts)


def ragged(key, count, total, bound, lean):
    if count == 2:
        one = jax.random.randint(key, (), max(1, total - bound), min(bound, total - 1) + 1)
        return jnp.stack([one, total - one])
    sizes = jnp.asarray(length_profile(count, total, bound, lean), jnp.int32)
    twos = (count - 1) // 2
    donor, receiver = sizes[1:1 + 2 * twos:2], sizes[2:2 + 2 * twos:2]
    slack = jnp.minimum(donor - 1, bound - receiver)
    moved = jax.random.randint(jax.random.fold_in(key, 1), (twos,), 0, 1 << 20) % (slack + 1)
    sizes = sizes.at[1:1 + 2 * twos:2].set(donor - moved).at[2:2 + 2 * twos:2].set(receiver + moved)
    return sizes[jax.random.permutation(jax.random.fold_in(key, 2), count)]


def scatter_about(own_key, shape, spread, bound, cuts=(), kind=jnp.bfloat16):
    entries = jax.random.normal(own_key, shape, jnp.float32) * spread
    if len(cuts) > 0:
        entries = level_of(own_key, shape, cuts, -0.22, 0.18) * entries
    return jnp.clip(entries, min=-bound, max=bound).astype(kind)


def setup_inputs(seed: int = 0) -> dict:
    key_of = jax.random.split(jax.random.key(seed), 5)
    return {
        "activations": draw_activations(jax.random.fold_in(key_of[4], 71), 0),
        "norm_gain": draw_norm_gain(jax.random.fold_in(key_of[4], 71), 0),
        "qkv_weight": scatter_about(key_of[2], (D, HEADS, 3 * HEAD_DIM), D ** -0.5, 0.09375, ((0, 2), (1, 4))),
        "doc_ids": jnp.searchsorted(jnp.cumsum(ragged(key_of[3], DOCS, TOKENS, DOC_MOST, 0)), jnp.arange(TOKENS), side="right").astype(jnp.int32),
    }


def rotate(vectors, places):
    half = vectors.shape[-1] // 2
    spacing = jnp.arange(half).astype(jnp.float32) * (2.0 / vectors.shape[-1])
    inverse = jnp.power(10000.0, -spacing)
    angles = places.astype(jnp.float32)[:, None] * inverse[None, :]
    cosine = jnp.cos(angles)[:, None, :]
    sine = jnp.sin(angles)[:, None, :]
    first_half = vectors[..., :half]
    second_half = vectors[..., half:]
    return jnp.concatenate([first_half * cosine - second_half * sine, first_half * sine + second_half * cosine], axis=-1)

def reference(activations, norm_gain, qkv_weight, doc_ids):
    widened = activations.astype(jnp.float32)
    mean_square = lax.optimization_barrier(jnp.mean(widened * widened, axis=1, keepdims=True))
    normed = (widened * lax.rsqrt(mean_square + 1e-05) * norm_gain.astype(jnp.float32)).astype(jnp.bfloat16)
    flat_weight = qkv_weight.reshape(D, HEADS * 3 * HEAD_DIM)
    projected = jnp.dot(normed, flat_weight, preferred_element_type=jnp.float32).reshape(TOKENS, HEADS, 3 * HEAD_DIM)
    places = jnp.arange(TOKENS).astype(jnp.int32)
    query = rotate(projected[..., :HEAD_DIM], places).astype(jnp.bfloat16)
    keys = rotate(projected[..., HEAD_DIM:2 * HEAD_DIM], places).astype(jnp.bfloat16)
    values = projected[..., 2 * HEAD_DIM:].astype(jnp.bfloat16)
    block = math.gcd(TOKENS, 512)
    scale = 1.0 / math.sqrt(HEAD_DIM)

    def one_head(operands):
        head_query, head_keys, head_values = operands

        def one_block(index):
            begin = index * block
            query_rows = lax.dynamic_slice_in_dim(head_query, begin, block, 0)
            query_places = begin + jnp.arange(block).astype(jnp.int32)
            query_docs = lax.dynamic_slice_in_dim(doc_ids, begin, block, 0)
            scores = jnp.dot(query_rows, head_keys.T, preferred_element_type=jnp.float32) * scale
            visible = (places[None, :] <= query_places[:, None]) & (doc_ids[None, :] == query_docs[:, None])
            masked = jnp.where(visible, scores, -jnp.inf)
            row_top = lax.optimization_barrier(jnp.max(masked, axis=1, keepdims=True))
            exponentials = jnp.where(visible, jnp.exp(masked - row_top), 0.0)
            weights = exponentials.astype(jnp.bfloat16)
            numerator = jnp.dot(weights, head_values, preferred_element_type=jnp.float32)
            return (numerator / lax.optimization_barrier(jnp.sum(exponentials, axis=1, keepdims=True))).astype(jnp.bfloat16)
        blocks = lax.map(one_block, jnp.arange(TOKENS // block).astype(jnp.int32))
        return blocks.reshape(TOKENS, HEAD_DIM)
    heads_out = lax.map(one_head, (query.transpose(1, 0, 2), keys.transpose(1, 0, 2), values.transpose(1, 0, 2)))
    return heads_out.transpose(1, 0, 2).reshape(TOKENS, HEADS * HEAD_DIM)
```

```python
import functools
import math

import jax
import jax.numpy as jnp
import numpy as np
from jax import lax
from jax.experimental import pallas as pl
from jax.experimental.pallas import tpu as pltpu
from jax.sharding import PartitionSpec as P

MESH = pl.DeviceIdType.MESH
F32 = jnp.float32
BF16 = jnp.bfloat16
NX, NY, NZ = 4, 4, 8
ROWS = 176
WIDTH = 1024
HALF = 2048
SUBS = 4
PIECE = 512 // SUBS
HIDE = -1e30
BIG = 1e9
PLUS = (0, 1)
MINUS = (3, 2)
ORDER = (0, 1, 3, 2)
SCALE = math.log2(math.e) / math.sqrt(128.0)


def kernel(
    x_ref, g_ref, w_ref, doc_ref, inv_ref, o_ref,
    xall, gall, wown, woth, cnt, cntall, bnd, xn, acc, cosb, sinb, stg, kv, qb, qcat, kaug,
    mrun, oacc, osend, obuf,
    lsem, wys, wyr, wzs, wzr, xs, xr, gs, gr, ps, pr, cs, cr, bs, br, as_, akr, aqr,
    rs, rp, rm, pks, pkr, os_, orr,
):
    t = lax.axis_index("tok")
    r = lax.axis_index("row")
    c = lax.axis_index("col")
    k = lax.rem(t, 2)
    yh = lax.rem(lax.div(t, 2), 2)
    z = lax.div(t, 4)
    y = yh * 2 + r
    zp = lax.rem(z, 2)

    def dev(cx, cy, cz, ck):
        return ((cz * 2 + lax.div(cy, 2)) * 2 + ck, lax.rem(cy, 2), cx)

    def xo(i):
        return lax.rem(c + i, NX)

    def yo(i):
        return lax.rem(y + i, NY)

    def zo(i):
        return lax.rem(z + i, NZ)

    partner = dev(c, y, z, 1 - k)
    pending = []

    def send(src, dst, ssem, rsem, to):
        copy = pltpu.make_async_remote_copy(
            src_ref=src, dst_ref=dst, send_sem=ssem, recv_sem=rsem,
            device_id=to, device_id_type=MESH,
        )
        copy.start()
        pending.append(copy)

    def landed(dst, rsem):
        pltpu.make_async_copy(dst, dst, rsem).wait()

    own_x = pltpu.make_async_copy(x_ref, xall.at[c, k], lsem.at[0])
    own_g = pltpu.make_async_copy(g_ref, gall.at[c], lsem.at[1])
    own_w = pltpu.make_async_copy(w_ref, wown, lsem.at[2])
    own_x.start()
    own_g.start()
    own_w.start()

    lane = lax.broadcasted_iota(jnp.int32, (1, 128), 1)
    ids = doc_ref[...]
    below = [jnp.sum((ids < d).astype(F32), axis=1, keepdims=True) for d in (1, 2, 3)]
    low = sum(jnp.where(lane == d + 1, below[d], 0.0) for d in range(3))
    high = sum(jnp.where(lane == d, below[d], 0.0) for d in range(3))
    sub = lax.broadcasted_iota(jnp.int32, (8, 128), 0)
    counts = jnp.where(sub == 0, low, jnp.where(sub == 1, high, 0.0))
    cnt[...] = counts
    cntall[0] = counts

    barrier = pltpu.get_barrier_semaphore()
    peers = [dev(xo(i), y, z, k) for i in (1, 2, 3)]
    peers += [dev(c, y, zo(1), k), dev(c, y, zo(NZ - 1), k)]
    plane = [(dy, dk) for dy in range(NY) for dk in range(2) if (dy, dk) != (0, 0)]
    core = (k, 1 - k)
    peers += [dev(c, yo(dy), z, core[dk]) for dy, dk in plane]
    for peer in peers:
        pl.semaphore_signal(barrier, inc=1, device_id=peer, device_id_type=MESH)
    pl.semaphore_wait(barrier, len(peers))

    yup, ydown = dev(c, yo(1), z, k), dev(c, yo(3), z, k)
    zup, zdown = dev(c, y, zo(1), k), dev(c, y, zo(NZ - 1), k)
    xup, xdown = dev(xo(1), y, z, k), dev(xo(3), y, z, k)
    for s in range(SUBS):
        for way, to in ((0, yup), (1, ydown)):
            off = way * 512 + s * PIECE
            send(
                w_ref.at[pl.ds(pl.multiple_of(zp * 1024 + off, PIECE), PIECE), :],
                woth.at[zp, pl.ds(off, PIECE), :],
                wys.at[way * SUBS + s], wyr.at[way * SUBS + s], to,
            )
        if s == 0:
            send(x_ref, xall.at[c, k], xs.at[0], xr.at[0], xup)
            send(x_ref, xall.at[c, k], xs.at[1], xr.at[1], xdown)
            send(x_ref, xall.at[c, k], ps.at[0], pr.at[0], partner)
            for i in (1, 2, 3):
                send(g_ref, gall.at[c], gs.at[i - 1], gr.at[NX - i - 1], dev(xo(i), y, z, k))
            for n, (dy, dk) in enumerate(plane):
                rel = ((NY - dy) % NY) * 2 + dk
                send(cnt, cntall.at[rel], cs.at[n], cr.at[rel - 1], dev(c, yo(dy), z, core[dk]))

    row = lax.broadcasted_iota(jnp.int32, (2 * ROWS, 128), 0)
    lanes = lax.broadcasted_iota(jnp.int32, (2 * ROWS, 128), 1)
    place = (z * 8 + yh * 4 + r) * ROWS + row + jnp.where(row >= ROWS, ROWS, 0)
    angle = place.astype(F32) * inv_ref[...]
    cosb[...] = jnp.cos(angle)
    sine = jnp.sin(angle)
    sinb[...] = jnp.where(lanes < 64, -sine, sine)

    for n in range(7):
        landed(cntall.at[n + 1], cr.at[n])
    total = cntall[0]
    for n in range(7):
        total = total + cntall[n + 1]
    lane8 = lax.broadcasted_iota(jnp.int32, (8, 128), 1)
    bnd[z] = jnp.where((sub == 1) & (lane8 >= 3), BIG, total)

    def forward_w(s):
        for way, to in ((0, zup), (1, zdown)):
            piece = woth.at[zp, pl.ds(way * 512 + s * PIECE, PIECE), :]
            landed(piece, wyr.at[way * SUBS + s])
            send(piece, piece, wzs.at[way * SUBS + s], wzr.at[way * SUBS + s], to)

    def bounds_hop(d):
        if d > 0:
            landed(bnd.at[zo(NZ - d)], br.at[2 * (d - 1)])
            if d < 4:
                landed(bnd.at[zo(d)], br.at[2 * (d - 1) + 1])
        if d < 4:
            send(bnd.at[zo(NZ - d)], bnd.at[zo(NZ - d)], bs.at[2 * d], br.at[2 * d], zup)
        if d < 3:
            send(bnd.at[zo(d)], bnd.at[zo(d)], bs.at[2 * d + 1], br.at[2 * d + 1], zdown)

    forward_w(0)
    bounds_hop(0)
    left, right, far = xo(3), xo(1), xo(2)
    landed(xall.at[left, k], xr.at[0])
    part = xall.at[left, k, pl.ds(0, 96), :]
    send(part, part, xs.at[2], xr.at[2], xup)
    send(xall.at[left, k], xall.at[left, k], ps.at[1], pr.at[1], partner)
    landed(xall.at[right, k], xr.at[1])
    part = xall.at[right, k, pl.ds(96, 80), :]
    send(part, part, xs.at[3], xr.at[3], xdown)
    send(xall.at[right, k], xall.at[right, k], ps.at[2], pr.at[2], partner)
    forward_w(1)
    bounds_hop(1)
    landed(xall.at[far, k, pl.ds(0, 96), :], xr.at[2])
    landed(xall.at[far, k, pl.ds(96, 80), :], xr.at[3])
    send(xall.at[far, k], xall.at[far, k], ps.at[3], pr.at[3], partner)
    forward_w(2)
    bounds_hop(2)

    own_x.wait()
    own_g.wait()
    for i in (1, 2, 3):
        landed(gall.at[xo(i)], gr.at[i - 1])
    for n, block in enumerate((c, left, right, far)):
        landed(xall.at[block, 1 - k], pr.at[n])
    for kk in range(2):
        squares = jnp.zeros((ROWS, 128), F32)
        for cc in range(NX):
            for s in range(8):
                v = xall[cc, kk, :, s * 128 : (s + 1) * 128].astype(F32)
                squares = squares + v * v
        mean = jnp.sum(squares, axis=1, keepdims=True) * (1.0 / (NX * WIDTH))
        inverse = jnp.broadcast_to(lax.rsqrt(mean + 1e-05), (ROWS, 128))
        for cc in range(NX):
            for s in range(8):
                v = xall[cc, kk, :, s * 128 : (s + 1) * 128].astype(F32)
                gain = gall[cc, s : s + 1, :].astype(F32)
                xn[cc, kk * ROWS : (kk + 1) * ROWS, s * 128 : (s + 1) * 128] = (
                    v * inverse * gain
                ).astype(BF16)
    forward_w(3)
    bounds_hop(3)

    own_w.wait()
    acc[...] = jnp.dot(xn[2 * r], wown[0:1024, :], preferred_element_type=F32)
    acc[...] += jnp.dot(xn[2 * r + 1], wown[1024:2048, :], preferred_element_type=F32)
    acc[...] += jnp.dot(xn[2 * (1 - r) + zp], woth[zp], preferred_element_type=F32)
    bounds_hop(4)
    for s in range(SUBS):
        for way in range(2):
            landed(
                woth.at[1 - zp, pl.ds(way * 512 + s * PIECE, PIECE), :],
                wzr.at[way * SUBS + s],
            )
    acc[...] += jnp.dot(xn[2 * (1 - r) + 1 - zp], woth[1 - zp], preferred_element_type=F32)

    def kv_at(p, zz, yy):
        return kv.at[p, zz, lax.div(yy, 2), pl.ds(0, 2), lax.rem(yy, 2)]

    cosine, sine = cosb[...], sinb[...]
    exchange = []
    for hh in range(2):
        for n in (1, 2, 0):
            u = acc[:, hh * 384 + n * 128 : hh * 384 + (n + 1) * 128]
            if n < 2:
                u = u * cosine + pltpu.roll(u, 64, 1) * sine
            stg[hh, n, 0] = u[:ROWS].astype(BF16)
            stg[hh, n, 1] = u[ROWS:].astype(BF16)
    for hh in range(2):
        yd = 2 * k + hh
        rel = lax.rem(y - yd + NY, NY)
        for j in range(2):
            here = jnp.logical_and(yd == y, k == j)
            to = dev(c, yd, z, j)
            moves = (
                (stg.at[hh, 1 + j], kv_at(j, z, y), as_.at[(hh * 2 + j) * 2], akr.at[rel]),
                (stg.at[hh, 0, j], qb.at[y], as_.at[(hh * 2 + j) * 2 + 1], aqr.at[rel]),
            )

            @pl.when(here)
            def _():
                for src, dst, _s, rsem in moves:
                    pltpu.make_async_copy(src, dst, rsem).start()

            @pl.when(jnp.logical_not(here))
            def _():
                for src, dst, ssem, rsem in moves:
                    pltpu.make_async_remote_copy(
                        src_ref=src, dst_ref=dst, send_sem=ssem, recv_sem=rsem,
                        device_id=to, device_id_type=MESH,
                    ).start()

            exchange.append((here, moves, to))

    for u in ORDER:
        block = kv_at(k, z, yo(u))
        landed(block, akr.at[u])
        send(block, block, rs.at[u], rp.at[u], zup)
        send(block, block, rs.at[4 + u], rm.at[u], zdown)
    send(kv.at[k, z], kv.at[k, z], pks.at[0], pkr.at[0], partner)

    mrun[...] = jnp.full_like(mrun, HIDE)
    oacc[...] = jnp.zeros_like(oacc)
    for u in ORDER:
        landed(qb.at[yo(u)], aqr.at[u])
    qrow = lax.broadcasted_iota(jnp.int32, (4 * ROWS, 128), 0)
    qplace = (qrow + jnp.where(qrow >= 2 * ROWS, 2 * ROWS, 0) + 2 * ROWS * k).astype(F32)
    mine = bnd[z]
    inside = (qplace >= mine[0:1, :]) & (qplace < mine[1:2, :])
    for n in range(4):
        qcat[n * ROWS : (n + 1) * ROWS, 0:128] = qb[n]
    qcat[:, 128:256] = jnp.where(inside, 1.0, 0.0).astype(BF16)

    def attend(zz, diagonal):
        limit = bnd[zz]
        krow = lax.broadcasted_iota(jnp.int32, (8 * ROWS, 128), 0).astype(F32)
        kin = (krow >= limit[0:1, :]) & (krow < limit[1:2, :])
        kaug[...] = jnp.where(kin, 0.0, HIDE).astype(BF16)

        def tile(i, carry):
            rows = pl.ds(pl.multiple_of(i * 2 * ROWS, 2 * ROWS), 2 * ROWS)
            keys = jnp.concatenate([kv[0, zz].reshape(8 * ROWS, 128), kaug[...]], axis=1)
            scores = lax.dot_general(
                qcat[rows, :], keys, (((1,), (1,)), ((), ())), preferred_element_type=F32
            ) * SCALE
            if diagonal:
                shape = (2 * ROWS, 8 * ROWS)
                qp = lax.broadcasted_iota(jnp.int32, shape, 0) + i * 4 * ROWS + 2 * ROWS * k
                kp = lax.broadcasted_iota(jnp.int32, shape, 1)
                scores = jnp.where(kp <= qp, scores, HIDE)
            before = mrun[rows, :]
            newest = jnp.maximum(before, jnp.max(scores, axis=1, keepdims=True))
            weights = jnp.exp2(scores - newest[:, 0:1]).astype(BF16)
            factor = jnp.exp2(before - newest)
            values = kv[1, zz].reshape(8 * ROWS, 128)
            values = jnp.concatenate([values, jnp.ones_like(values)], axis=1)
            added = jnp.dot(weights, values, preferred_element_type=F32)
            oacc[rows, :] = oacc[rows, :] * jnp.concatenate([factor, factor], axis=1) + added
            mrun[rows, :] = newest
            return carry

        lax.fori_loop(0, 2, tile, 0)

    landed(kv.at[1 - k, z], pkr.at[0])
    attend(z, True)

    for d in (1, 2, 3, 4):
        up, down = zo(NZ - d), zo(d)
        for u in ORDER:
            if d < 4 or u in PLUS:
                block = kv_at(k, up, yo(u))
                landed(block, rp.at[(d - 1) * 4 + u])
                if d < 3 or (d == 3 and u in PLUS):
                    send(block, block, rs.at[d * 8 + u], rp.at[d * 4 + u], zup)
            if d < 4 or u in MINUS:
                block = kv_at(k, down, yo(u))
                landed(block, rm.at[(d - 1) * 4 + u])
                if d < 3 or (d == 3 and u in MINUS):
                    send(block, block, rs.at[d * 8 + 4 + u], rm.at[d * 4 + u], zdown)
        send(kv.at[k, up], kv.at[k, up], pks.at[2 * d - 1], pkr.at[2 * d - 1], partner)
        if d < 4:
            send(kv.at[k, down], kv.at[k, down], pks.at[2 * d], pkr.at[2 * d], partner)
        landed(kv.at[1 - k, up], pkr.at[2 * d - 1])

        @pl.when(z >= d)
        def _():
            attend(up, False)

        if d < 4:
            landed(kv.at[1 - k, down], pkr.at[2 * d])

            @pl.when(z + d >= NZ)
            def _():
                attend(down, False)

    result = (oacc[:, 0:128] / oacc[:, 128:256]).astype(BF16)
    for n in range(4):
        osend[n] = result[n * ROWS : (n + 1) * ROWS]
    obuf[y] = osend[y]
    for dy in (1, 2, 3):
        send(osend.at[yo(dy)], obuf.at[y], os_.at[dy - 1], orr.at[NY - dy - 1], dev(c, yo(dy), z, k))
    for dy in (1, 2, 3):
        landed(obuf.at[yo(dy)], orr.at[dy - 1])
    for h in range(4):
        o_ref[:, h * 128 : (h + 1) * 128] = obuf[h]

    for here, moves, to in exchange:

        @pl.when(jnp.logical_not(here))
        def _():
            for src, dst, ssem, rsem in moves:
                pltpu.make_async_remote_copy(
                    src_ref=src, dst_ref=dst, send_sem=ssem, recv_sem=rsem,
                    device_id=to, device_id_type=MESH,
                ).wait_send()

    for copy in pending:
        copy.wait_send()


def per_device(activations, norm_gain, qkv_weight, doc_ids):
    core = lax.rem(lax.axis_index("tok"), 2)
    mine = lax.dynamic_slice_in_dim(qkv_weight, 2 * core, 2, axis=1).reshape(HALF, 768)
    spacing = np.arange(64).astype(np.float32) * np.float32(2.0 / 128)
    inverse = np.power(np.float32(10000.0), -spacing).astype(np.float32)
    inverse = np.concatenate([inverse, inverse])[None, :]
    dma = pltpu.SemaphoreType.DMA
    anywhere = pl.BlockSpec(memory_space=pl.ANY)
    local = pl.BlockSpec(memory_space=pltpu.VMEM)
    scratch = [
        pltpu.VMEM((NX, 2, ROWS, WIDTH), BF16),
        pltpu.VMEM((NX, 8, 128), BF16),
        pltpu.VMEM((HALF, 768), BF16),
        pltpu.VMEM((2, 1024, 768), BF16),
        pltpu.VMEM((8, 128), F32),
        pltpu.VMEM((8, 8, 128), F32),
        pltpu.VMEM((NZ, 8, 128), F32),
        pltpu.VMEM((NX, 2 * ROWS, WIDTH), BF16),
        pltpu.VMEM((2 * ROWS, 768), F32),
        pltpu.VMEM((2 * ROWS, 128), F32),
        pltpu.VMEM((2 * ROWS, 128), F32),
        pltpu.VMEM((2, 3, 2, ROWS, 128), BF16),
        pltpu.VMEM((2, NZ, 2, 2, 2, ROWS, 128), BF16),
        pltpu.VMEM((NY, ROWS, 128), BF16),
        pltpu.VMEM((4 * ROWS, 256), BF16),
        pltpu.VMEM((8 * ROWS, 128), BF16),
        pltpu.VMEM((4 * ROWS, 128), F32),
        pltpu.VMEM((4 * ROWS, 256), F32),
        pltpu.VMEM((NY, ROWS, 128), BF16),
        pltpu.VMEM((NY, ROWS, 128), BF16),
        dma((3,)),
        dma((2 * SUBS,)), dma((2 * SUBS,)),
        dma((2 * SUBS,)), dma((2 * SUBS,)),
        dma((4,)), dma((4,)),
        dma((3,)), dma((3,)),
        dma((4,)), dma((4,)),
        dma((7,)), dma((7,)),
        dma((8,)), dma((8,)),
        dma((8,)), dma((4,)), dma((4,)),
        dma((32,)), dma((16,)), dma((16,)),
        dma((8,)), dma((8,)),
        dma((3,)), dma((3,)),
    ]
    return pl.pallas_call(
        kernel,
        out_shape=jax.ShapeDtypeStruct((ROWS, 512), BF16),
        in_specs=[anywhere, anywhere, anywhere, local, local],
        out_specs=local,
        scratch_shapes=scratch,
        compiler_params=pltpu.CompilerParams(
            collective_id=0, has_side_effects=True, vmem_limit_bytes=60 * 1024 * 1024
        ),
        name="attention_block",
    )(
        activations, norm_gain.reshape(8, 128), mine, doc_ids.reshape(1, ROWS), jnp.asarray(inverse)
    )


def solution(mesh):
    placed = (P(("tok", "row"), "col"), P("col"), P("row", "col", None), P(("tok", "row")))
    return jax.shard_map(
        per_device, mesh=mesh, in_specs=placed, out_specs=P(("tok", "row"), "col"), check_vma=False
    )
```

```python
import functools
import math

import jax
import jax.numpy as jnp
import numpy as np
from jax import lax
from jax.experimental import pallas as pl
from jax.experimental.pallas import tpu as pltpu
from jax.sharding import PartitionSpec as P

MESH = pl.DeviceIdType.MESH
F32 = jnp.float32
BF16 = jnp.bfloat16
NX, NY, NZ = 4, 4, 8
ROWS = 176
WIDTH = 1024
HALF = 2048
SUBS = 4
PIECE = 512 // SUBS
QSUBS = 4
QPIECE = 1024 // QSUBS
HIDE = -1e30
BIG = 1e9
PLUS = (0, 1)
MINUS = (3, 2)
ORDER = (0, 1, 3, 2)
SCALE = math.log2(math.e) / math.sqrt(128.0)


def kernel(
    x_ref, g_ref, w_ref, doc_ref, inv_ref, o_ref,
    xall, gall, wkvo, wkvx, wqo, wqx, cnt, cntall, bnd, xn, acc, accq, cosb, sinb, stg, stgq, kv, qb, qcat, kaug,
    mrun, oacc, osend, obuf,
    lsem, wys, wyr, wzs, wzr, wqs, wqr, xs, xr, gs, gr, ps, pr, cs, cr, bs, br, as_, akr, aqs, aqr,
    rs, rp, rm, pks, pkr, os_, orr,
):
    t = lax.axis_index("tok")
    r = lax.axis_index("row")
    c = lax.axis_index("col")
    k = lax.rem(t, 2)
    yh = lax.rem(lax.div(t, 2), 2)
    z = lax.div(t, 4)
    y = yh * 2 + r
    zp = lax.rem(z, 2)

    def dev(cx, cy, cz, ck):
        return ((cz * 2 + lax.div(cy, 2)) * 2 + ck, lax.rem(cy, 2), cx)

    def xo(i):
        return lax.rem(c + i, NX)

    def yo(i):
        return lax.rem(y + i, NY)

    def zo(i):
        return lax.rem(z + i, NZ)

    partner = dev(c, y, z, 1 - k)
    pending = []

    def send(src, dst, ssem, rsem, to):
        copy = pltpu.make_async_remote_copy(
            src_ref=src, dst_ref=dst, send_sem=ssem, recv_sem=rsem,
            device_id=to, device_id_type=MESH,
        )
        copy.start()
        pending.append(copy)

    def landed(dst, rsem):
        pltpu.make_async_copy(dst, dst, rsem).wait()

    own_x = pltpu.make_async_copy(x_ref, xall.at[c, k], lsem.at[0])
    own_g = pltpu.make_async_copy(g_ref, gall.at[c], lsem.at[1])
    def q_columns(hh):
        return pl.ds(pl.multiple_of((2 * k + hh) * 384, 128), 128)

    def kv_columns(hh):
        return pl.ds(pl.multiple_of((2 * k + hh) * 384 + 128, 128), 256)

    own_w = []
    for hh in range(2):
        own_w.append(pltpu.make_async_copy(w_ref.at[:, kv_columns(hh)], wkvo.at[hh], lsem.at[2 + hh]))
    for hh in range(2):
        own_w.append(
            pltpu.make_async_copy(
                w_ref.at[:, q_columns(hh)], wqo.at[:, hh * 128 : (hh + 1) * 128], lsem.at[4 + hh]
            )
        )
    own_x.start()
    own_g.start()
    for copy in own_w:
        copy.start()

    lane = lax.broadcasted_iota(jnp.int32, (1, 128), 1)
    ids = doc_ref[...]
    below = [jnp.sum((ids < d).astype(F32), axis=1, keepdims=True) for d in (1, 2, 3)]
    low = sum(jnp.where(lane == d + 1, below[d], 0.0) for d in range(3))
    high = sum(jnp.where(lane == d, below[d], 0.0) for d in range(3))
    sub = lax.broadcasted_iota(jnp.int32, (8, 128), 0)
    counts = jnp.where(sub == 0, low, jnp.where(sub == 1, high, 0.0))
    cnt[...] = counts
    cntall[0] = counts

    barrier = pltpu.get_barrier_semaphore()
    peers = [dev(xo(i), y, z, k) for i in (1, 2, 3)]
    peers += [dev(c, y, zo(1), k), dev(c, y, zo(NZ - 1), k)]
    plane = [(dy, dk) for dy in range(NY) for dk in range(2) if (dy, dk) != (0, 0)]
    core = (k, 1 - k)
    peers += [dev(c, yo(dy), z, core[dk]) for dy, dk in plane]
    for peer in peers:
        pl.semaphore_signal(barrier, inc=1, device_id=peer, device_id_type=MESH)
    pl.semaphore_wait(barrier, len(peers))

    yup, ydown = dev(c, yo(1), z, k), dev(c, yo(3), z, k)
    zup, zdown = dev(c, y, zo(1), k), dev(c, y, zo(NZ - 1), k)
    xup, xdown = dev(xo(1), y, z, k), dev(xo(3), y, z, k)
    for i in (1, 2, 3):
        send(g_ref, gall.at[c], gs.at[i - 1], gr.at[NX - i - 1], dev(xo(i), y, z, k))
    for n, (dy, dk) in enumerate(plane):
        rel = ((NY - dy) % NY) * 2 + dk
        send(cnt, cntall.at[rel], cs.at[n], cr.at[rel - 1], dev(c, yo(dy), z, core[dk]))
    cuts = (pl.ds(0, 48), pl.ds(48, 48), pl.ds(96, 48), pl.ds(144, 32))

    def send_wkv(s):
        for hh in range(2):
            for way, to in ((0, yup), (1, ydown)):
                off = way * 512 + s * PIECE
                n = (way * SUBS + s) * 2 + hh
                send(
                    w_ref.at[pl.ds(pl.multiple_of(zp * 1024 + off, PIECE), PIECE), kv_columns(hh)],
                    wkvx.at[zp, hh, pl.ds(off, PIECE), :], wys.at[n], wyr.at[n], to,
                )

    def send_x(i):
        send(x_ref.at[cuts[i], :], xall.at[c, k, cuts[i], :], xs.at[i], xr.at[i], xup)
        i = 3 - i
        send(x_ref.at[cuts[i], :], xall.at[c, k, cuts[i], :], xs.at[4 + i], xr.at[4 + i], xdown)

    left, right, far = xo(3), xo(1), xo(2)

    def relay_x(i):
        part = xall.at[left, k, cuts[i], :]
        landed(part, xr.at[i])
        send(part, part, xs.at[8 + i], xr.at[8 + i], xup)
        i = 3 - i
        part = xall.at[right, k, cuts[i], :]
        landed(part, xr.at[4 + i])
        send(part, part, xs.at[8 + i], xr.at[8 + i], xdown)

    for i in range(2):
        send_wkv(i)
        send_x(i)
    send_x(2)
    send_x(3)
    send(x_ref, xall.at[c, k], ps.at[0], pr.at[0], partner)

    def send_wq(s):
        for way, to in ((0, yup), (1, ydown)):
            for hh in range(2):
                rows = pl.ds(way * 1024 + s * QPIECE, QPIECE)
                n = (way * QSUBS + s) * 2 + hh
                send(
                    w_ref.at[rows, q_columns(hh)], wqx.at[rows, hh * 128 : (hh + 1) * 128],
                    wqs.at[n], wqr.at[n], to,
                )

    row = lax.broadcasted_iota(jnp.int32, (2 * ROWS, 128), 0)
    lanes = lax.broadcasted_iota(jnp.int32, (2 * ROWS, 128), 1)
    place = (z * 8 + yh * 4 + r) * ROWS + row + jnp.where(row >= ROWS, ROWS, 0)
    angle = place.astype(F32) * inv_ref[...]
    cosb[...] = jnp.cos(angle)
    sine = jnp.sin(angle)
    sinb[...] = jnp.where(lanes < 64, -sine, sine)

    for n in range(7):
        landed(cntall.at[n + 1], cr.at[n])
    total = cntall[0]
    for n in range(7):
        total = total + cntall[n + 1]
    lane8 = lax.broadcasted_iota(jnp.int32, (8, 128), 1)
    bnd[z] = jnp.where((sub == 1) & (lane8 >= 3), BIG, total)

    def forward_w(s):
        for way, to in ((0, zup), (1, zdown)):
            rows = pl.ds(way * 512 + s * PIECE, PIECE)
            for hh in range(2):
                landed(wkvx.at[zp, hh, rows, :], wyr.at[(way * SUBS + s) * 2 + hh])
            piece = wkvx.at[zp, pl.ds(0, 2), rows, :]
            send(piece, piece, wzs.at[way * SUBS + s], wzr.at[way * SUBS + s], to)

    def bounds_hop(d):
        if d > 0:
            landed(bnd.at[zo(NZ - d)], br.at[2 * (d - 1)])
            if d < 4:
                landed(bnd.at[zo(d)], br.at[2 * (d - 1) + 1])
        if d < 4:
            send(bnd.at[zo(NZ - d)], bnd.at[zo(NZ - d)], bs.at[2 * d], br.at[2 * d], zup)
        if d < 3:
            send(bnd.at[zo(d)], bnd.at[zo(d)], bs.at[2 * d + 1], br.at[2 * d + 1], zdown)

    forward_w(0)
    send_wkv(2)
    bounds_hop(0)
    relay_x(0)
    relay_x(1)
    forward_w(1)
    send_wkv(3)
    bounds_hop(1)
    for i in (2, 3):
        landed(xall.at[left, k, cuts[i], :], xr.at[i])
        landed(xall.at[right, k, cuts[3 - i], :], xr.at[7 - i])
    send(xall.at[left, k], xall.at[left, k], ps.at[1], pr.at[1], partner)
    send(xall.at[right, k], xall.at[right, k], ps.at[2], pr.at[2], partner)
    forward_w(2)
    send_wq(0)
    bounds_hop(2)
    for i in range(4):
        landed(xall.at[far, k, cuts[i], :], xr.at[8 + i])
    send(xall.at[far, k], xall.at[far, k], ps.at[3], pr.at[3], partner)
    own_x.wait()
    own_g.wait()
    for i in (1, 2, 3):
        landed(gall.at[xo(i)], gr.at[i - 1])

    def normalise(kk, at):
        squares = jnp.zeros((ROWS, 128), F32)
        for cc in range(NX):
            for s in range(8):
                v = xall[cc, kk, :, s * 128 : (s + 1) * 128].astype(F32)
                squares = squares + v * v
        mean = jnp.sum(squares, axis=1, keepdims=True) * (1.0 / (NX * WIDTH))
        inverse = jnp.broadcast_to(lax.rsqrt(mean + 1e-05), (ROWS, 128))
        for cc in range(NX):
            for s in range(8):
                v = xall[cc, kk, :, s * 128 : (s + 1) * 128].astype(F32)
                gain = gall[cc, s : s + 1, :].astype(F32)
                xn[cc, at, s * 128 : (s + 1) * 128] = (v * inverse * gain).astype(BF16)

    normalise(k, pl.ds(pl.multiple_of(k * ROWS, ROWS), ROWS))
    forward_w(3)
    send_wq(1)
    bounds_hop(3)
    for n, block in enumerate((c, left, right, far)):
        landed(xall.at[block, 1 - k], pr.at[n])
    normalise(1 - k, pl.ds(pl.multiple_of((1 - k) * ROWS, ROWS), ROWS))
    for hh in range(2):
        own_w[hh].wait()
        out = slice(hh * 256, (hh + 1) * 256)
        acc[:, out] = jnp.dot(xn[2 * r], wkvo[hh, 0:1024], preferred_element_type=F32)
        acc[:, out] += jnp.dot(xn[2 * r + 1], wkvo[hh, 1024:2048], preferred_element_type=F32)
        acc[:, out] += jnp.dot(xn[2 * (1 - r) + zp], wkvx[zp, hh], preferred_element_type=F32)
    bounds_hop(4)
    for s in range(SUBS):
        for way in range(2):
            landed(
                wkvx.at[1 - zp, pl.ds(0, 2), pl.ds(way * 512 + s * PIECE, PIECE), :],
                wzr.at[way * SUBS + s],
            )
    for hh in range(2):
        out = slice(hh * 256, (hh + 1) * 256)
        acc[:, out] += jnp.dot(xn[2 * (1 - r) + 1 - zp], wkvx[1 - zp, hh], preferred_element_type=F32)

    def kv_at(p, zz, yy):
        return kv.at[p, zz, lax.div(yy, 2), pl.ds(0, 2), lax.rem(yy, 2)]

    for hh in range(2):
        u = acc[:, hh * 256 : hh * 256 + 128]
        u = u * cosb[...] + pltpu.roll(u, 64, 1) * sinb[...]
        stg[hh, 0, 0] = u[:ROWS].astype(BF16)
        stg[hh, 0, 1] = u[ROWS:].astype(BF16)
        u = acc[:, hh * 256 + 128 : hh * 256 + 256]
        stg[hh, 1, 0] = u[:ROWS].astype(BF16)
        stg[hh, 1, 1] = u[ROWS:].astype(BF16)
    exchange = []

    def exchange_send(source, slot_of, ssems, rsems):
        for hh in range(2):
            yd = 2 * k + hh
            rel = lax.rem(y - yd + NY, NY)
            for j in range(2):
                here = jnp.logical_and(yd == y, k == j)
                to = dev(c, yd, z, j)
                move = (source.at[hh, j], slot_of(j), ssems.at[hh * 2 + j], rsems.at[rel])

                @pl.when(here)
                def _():
                    pltpu.make_async_copy(move[0], move[1], move[3]).start()

                @pl.when(jnp.logical_not(here))
                def _():
                    pltpu.make_async_remote_copy(
                        src_ref=move[0], dst_ref=move[1], send_sem=move[2], recv_sem=move[3],
                        device_id=to, device_id_type=MESH,
                    ).start()

                exchange.append((here, move, to))

    exchange_send(stg, lambda j: kv_at(j, z, y), as_, akr)
    send_wq(2)
    send_wq(3)

    own_w[2].wait()
    own_w[3].wait()
    accq[...] = jnp.dot(xn[2 * r], wqo[0:1024, :], preferred_element_type=F32)
    accq[...] += jnp.dot(xn[2 * r + 1], wqo[1024:2048, :], preferred_element_type=F32)

    def project_q(part):
        for s in (2 * part, 2 * part + 1):
            for way in range(2):
                for hh in range(2):
                    landed(
                        wqx.at[pl.ds(way * 1024 + s * QPIECE, QPIECE), hh * 128 : (hh + 1) * 128],
                        wqr.at[(way * QSUBS + s) * 2 + hh],
                    )
        low = part * 512
        for way in range(2):
            accq[...] += jnp.dot(
                xn[2 * (1 - r) + way, :, low : low + 512],
                wqx[way * 1024 + low : way * 1024 + low + 512, :],
                preferred_element_type=F32,
            )

    project_q(0)
    for u in ORDER:
        block = kv_at(k, z, yo(u))
        landed(block, akr.at[u])
        send(block, block, rs.at[u], rp.at[u], zup)
        send(block, block, rs.at[4 + u], rm.at[u], zdown)
        send(block, block, pks.at[u], pkr.at[u], partner)

    def ring(d, pieces):
        up, down = zo(NZ - d), zo(d)
        for u in pieces:
            if d < 4 or u in PLUS:
                block = kv_at(k, up, yo(u))
                landed(block, rp.at[(d - 1) * 4 + u])
                if d < 3 or (d == 3 and u in PLUS):
                    send(block, block, rs.at[d * 8 + u], rp.at[d * 4 + u], zup)
                n = (2 * d - 1) * 4 + u
                send(block, block, pks.at[n], pkr.at[n], partner)
            if d < 4 or u in MINUS:
                block = kv_at(k, down, yo(u))
                landed(block, rm.at[(d - 1) * 4 + u])
                if d < 3 or (d == 3 and u in MINUS):
                    send(block, block, rs.at[d * 8 + 4 + u], rm.at[d * 4 + u], zdown)
                n = (2 * d if d < 4 else 7) * 4 + u
                send(block, block, pks.at[n], pkr.at[n], partner)
    project_q(1)
    for hh in range(2):
        u = accq[:, hh * 128 : (hh + 1) * 128]
        u = u * cosb[...] + pltpu.roll(u, 64, 1) * sinb[...]
        stgq[hh, 0] = u[:ROWS].astype(BF16)
        stgq[hh, 1] = u[ROWS:].astype(BF16)
    exchange_send(stgq, lambda j: qb.at[y], aqs, aqr)

    ring(1, ORDER)

    mrun[...] = jnp.full_like(mrun, HIDE)
    oacc[...] = jnp.zeros_like(oacc)
    qrow = lax.broadcasted_iota(jnp.int32, (4 * ROWS, 128), 0)
    qplace = (qrow + jnp.where(qrow >= 2 * ROWS, 2 * ROWS, 0) + 2 * ROWS * k).astype(F32)
    mine = bnd[z]
    inside = (qplace >= mine[0:1, :]) & (qplace < mine[1:2, :])
    qcat[:, 128:256] = jnp.where(inside, 1.0, 0.0).astype(BF16)
    for u in ORDER:
        landed(qb.at[yo(u)], aqr.at[u])
    for n in range(4):
        qcat[n * ROWS : (n + 1) * ROWS, 0:128] = qb[n]

    def attend(zz, diagonal):
        limit = bnd[zz]
        krow = lax.broadcasted_iota(jnp.int32, (8 * ROWS, 128), 0).astype(F32)
        kin = (krow >= limit[0:1, :]) & (krow < limit[1:2, :])
        kaug[...] = jnp.where(kin, 0.0, HIDE).astype(BF16)

        keys = jnp.concatenate([kv[0, zz].reshape(8 * ROWS, 128), kaug[...]], axis=1)
        values = kv[1, zz].reshape(8 * ROWS, 128)
        values = jnp.concatenate([values, jnp.ones_like(values)], axis=1)

        def scored(i):
            rows = slice(i * 2 * ROWS, (i + 1) * 2 * ROWS)
            return lax.dot_general(
                qcat[rows, :], keys, (((1,), (1,)), ((), ())), preferred_element_type=F32
            )

        def absorb(i, scores):
            rows = slice(i * 2 * ROWS, (i + 1) * 2 * ROWS)
            if diagonal:
                shape = (2 * ROWS, 8 * ROWS)
                qp = lax.broadcasted_iota(jnp.int32, shape, 0) + i * 4 * ROWS + 2 * ROWS * k
                kp = lax.broadcasted_iota(jnp.int32, shape, 1)
                scores = jnp.where(kp <= qp, scores, HIDE)
            before = mrun[rows, :]
            newest = jnp.maximum(before, jnp.max(scores, axis=1, keepdims=True))
            weights = jnp.exp2((scores - newest[:, 0:1]) * SCALE).astype(BF16)
            factor = jnp.exp2((before - newest) * SCALE)
            added = jnp.dot(weights, values, preferred_element_type=F32)
            oacc[rows, :] = oacc[rows, :] * jnp.concatenate([factor, factor], axis=1) + added
            mrun[rows, :] = newest

        first = scored(0)
        second = scored(1)
        absorb(0, first)
        absorb(1, second)

    def shared(zz, n):
        for u in ORDER:
            landed(kv_at(1 - k, zz, yo(u)), pkr.at[n * 4 + u])

    def attend_up(d):
        shared(zo(NZ - d), 2 * d - 1)

        @pl.when(z >= d)
        def _():
            attend(zo(NZ - d), False)

    def attend_down(d):
        shared(zo(d), 2 * d)

        @pl.when(z + d >= NZ)
        def _():
            attend(zo(d), False)

    shared(z, 0)
    attend(z, True)
    ring(2, ORDER)
    attend_up(1)
    attend_down(1)
    ring(3, ORDER[:2])
    attend_up(2)
    ring(3, ORDER[2:])
    attend_down(2)
    ring(4, ORDER)
    attend_up(3)
    attend_down(3)
    attend_up(4)

    result = (oacc[:, 0:128] / oacc[:, 128:256]).astype(BF16)
    for n in range(4):
        osend[n] = result[n * ROWS : (n + 1) * ROWS]
    obuf[y] = osend[y]
    for dy in (1, 2, 3):
        send(osend.at[yo(dy)], obuf.at[y], os_.at[dy - 1], orr.at[NY - dy - 1], dev(c, yo(dy), z, k))
    for dy in (1, 2, 3):
        landed(obuf.at[yo(dy)], orr.at[dy - 1])
    for h in range(4):
        o_ref[:, h * 128 : (h + 1) * 128] = obuf[h]

    for here, move, to in exchange:

        @pl.when(jnp.logical_not(here))
        def _():
            pltpu.make_async_remote_copy(
                src_ref=move[0], dst_ref=move[1], send_sem=move[2], recv_sem=move[3],
                device_id=to, device_id_type=MESH,
            ).wait_send()

    for copy in pending:
        copy.wait_send()


def per_device(activations, norm_gain, qkv_weight, doc_ids):
    mine = qkv_weight.reshape(HALF, 1536)
    spacing = np.arange(64).astype(np.float32) * np.float32(2.0 / 128)
    inverse = np.power(np.float32(10000.0), -spacing).astype(np.float32)
    inverse = np.concatenate([inverse, inverse])[None, :]
    dma = pltpu.SemaphoreType.DMA
    anywhere = pl.BlockSpec(memory_space=pl.ANY)
    local = pl.BlockSpec(memory_space=pltpu.VMEM)
    scratch = [
        pltpu.VMEM((NX, 2, ROWS, WIDTH), BF16),
        pltpu.VMEM((NX, 8, 128), BF16),
        pltpu.VMEM((2, HALF, 256), BF16),
        pltpu.VMEM((2, 2, 1024, 256), BF16),
        pltpu.VMEM((HALF, 256), BF16),
        pltpu.VMEM((HALF, 256), BF16),
        pltpu.VMEM((8, 128), F32),
        pltpu.VMEM((8, 8, 128), F32),
        pltpu.VMEM((NZ, 8, 128), F32),
        pltpu.VMEM((NX, 2 * ROWS, WIDTH), BF16),
        pltpu.VMEM((2 * ROWS, 512), F32),
        pltpu.VMEM((2 * ROWS, 256), F32),
        pltpu.VMEM((2 * ROWS, 128), F32),
        pltpu.VMEM((2 * ROWS, 128), F32),
        pltpu.VMEM((2, 2, 2, ROWS, 128), BF16),
        pltpu.VMEM((2, 2, ROWS, 128), BF16),
        pltpu.VMEM((2, NZ, 2, 2, 2, ROWS, 128), BF16),
        pltpu.VMEM((NY, ROWS, 128), BF16),
        pltpu.VMEM((4 * ROWS, 256), BF16),
        pltpu.VMEM((8 * ROWS, 128), BF16),
        pltpu.VMEM((4 * ROWS, 128), F32),
        pltpu.VMEM((4 * ROWS, 256), F32),
        pltpu.VMEM((NY, ROWS, 128), BF16),
        pltpu.VMEM((NY, ROWS, 128), BF16),
        dma((6,)),
        dma((4 * SUBS,)), dma((4 * SUBS,)),
        dma((2 * SUBS,)), dma((2 * SUBS,)),
        dma((4 * QSUBS,)), dma((4 * QSUBS,)),
        dma((12,)), dma((12,)),
        dma((3,)), dma((3,)),
        dma((4,)), dma((4,)),
        dma((7,)), dma((7,)),
        dma((8,)), dma((8,)),
        dma((4,)), dma((4,)), dma((4,)), dma((4,)),
        dma((32,)), dma((16,)), dma((16,)),
        dma((32,)), dma((32,)),
        dma((3,)), dma((3,)),
    ]
    return pl.pallas_call(
        kernel,
        out_shape=jax.ShapeDtypeStruct((ROWS, 512), BF16),
        in_specs=[anywhere, anywhere, anywhere, local, local],
        out_specs=local,
        scratch_shapes=scratch,
        compiler_params=pltpu.CompilerParams(
            collective_id=0, has_side_effects=True, vmem_limit_bytes=60 * 1024 * 1024
        ),
        name="attention_block",
    )(
        activations, norm_gain.reshape(8, 128), mine, doc_ids.reshape(1, ROWS), jnp.asarray(inverse)
    )


def solution(mesh):
    placed = (P(("tok", "row"), "col"), P("col"), P("row", "col", None), P(("tok", "row")))
    return jax.shard_map(
        per_device, mesh=mesh, in_specs=placed, out_specs=P(("tok", "row"), "col"), check_vma=False
    )
```

```python
import functools
import math

import jax
import jax.numpy as jnp
import numpy as np
from jax import lax
from jax.experimental import pallas as pl
from jax.experimental.pallas import tpu as pltpu
from jax.sharding import PartitionSpec as P

MESH = pl.DeviceIdType.MESH
F32 = jnp.float32
BF16 = jnp.bfloat16
NX, NY, NZ = 4, 4, 8
ROWS = 176
WIDTH = 1024
HALF = 2048
SUBS = 4
PIECE = 512 // SUBS
QSUBS = 4
QPIECE = 1024 // QSUBS
HIDE = -1e30
BIG = 1e9
PLUS = (0, 1)
MINUS = (3, 2)
ORDER = (0, 1, 3, 2)
SCALE = math.log2(math.e) / math.sqrt(128.0)


def kernel(
    x_ref, g_ref, w_ref, doc_ref, inv_ref, o_ref,
    xall, gall, raw, wkvo, wkvx, wqo, wqx, cnt, cntall, bnd, xn, acc, accq, cosb, sinb, stg, stgq, kv, qb, qcat, kaug,
    mrun, oacc, osend, obuf,
    lsem, wys, wyr, wzs, wzr, wqs, wqr, xs, xr, gs, gr, ps, pr, cs, cr, bs, br, as_, akr, aqs, aqr,
    rs, rp, rm, pks, pkr, os_, orr,
):
    t = lax.axis_index("tok")
    r = lax.axis_index("row")
    c = lax.axis_index("col")
    k = lax.rem(t, 2)
    yh = lax.rem(lax.div(t, 2), 2)
    z = lax.div(t, 4)
    y = yh * 2 + r
    zp = lax.rem(z, 2)

    def dev(cx, cy, cz, ck):
        return ((cz * 2 + lax.div(cy, 2)) * 2 + ck, lax.rem(cy, 2), cx)

    def xo(i):
        return lax.rem(c + i, NX)

    def yo(i):
        return lax.rem(y + i, NY)

    def zo(i):
        return lax.rem(z + i, NZ)

    partner = dev(c, y, z, 1 - k)
    pending = []

    def send(src, dst, ssem, rsem, to):
        copy = pltpu.make_async_remote_copy(
            src_ref=src, dst_ref=dst, send_sem=ssem, recv_sem=rsem,
            device_id=to, device_id_type=MESH,
        )
        copy.start()
        pending.append(copy)

    def landed(dst, rsem):
        pltpu.make_async_copy(dst, dst, rsem).wait()

    own_x = pltpu.make_async_copy(x_ref, xall.at[c, k], lsem.at[0])
    own_g = pltpu.make_async_copy(g_ref, gall.at[c], lsem.at[1])
    def raw_rows(n):
        half = zp if n < 8 else 1 - zp
        off = (n % 2) * 512 + (n % 8) // 2 * 128
        return pl.ds(pl.multiple_of(half * 1024 + off, 128), 128)

    raw_copies = [
        pltpu.make_async_copy(w_ref.at[raw_rows(n)], raw.at[raw_rows(n)], lsem.at[2 + n])
        for n in range(16)
    ]
    for copy in raw_copies:
        copy.start()
    own_x.start()
    own_g.start()

    def unpack_w(n):
        raw_copies[n].wait()
        rows = raw_rows(n)
        heads = jnp.swapaxes(raw[rows], 0, 1)
        for hh in range(2):
            head = jnp.where(k == 0, heads[hh], heads[2 + hh])
            wqo[rows, hh * 128 : (hh + 1) * 128] = head[:, 0:128]
            wkvo[hh, rows, :] = head[:, 128:384]


    lane = lax.broadcasted_iota(jnp.int32, (1, 128), 1)
    ids = doc_ref[...]
    below = [jnp.sum((ids < d).astype(F32), axis=1, keepdims=True) for d in (1, 2, 3)]
    low = sum(jnp.where(lane == d + 1, below[d], 0.0) for d in range(3))
    high = sum(jnp.where(lane == d, below[d], 0.0) for d in range(3))
    sub = lax.broadcasted_iota(jnp.int32, (8, 128), 0)
    counts = jnp.where(sub == 0, low, jnp.where(sub == 1, high, 0.0))
    cnt[...] = counts
    cntall[0] = counts

    barrier = pltpu.get_barrier_semaphore()
    peers = [dev(xo(i), y, z, k) for i in (1, 2, 3)]
    peers += [dev(c, y, zo(1), k), dev(c, y, zo(NZ - 1), k)]
    plane = [(dy, dk) for dy in range(NY) for dk in range(2) if (dy, dk) != (0, 0)]
    core = (k, 1 - k)
    peers += [dev(c, yo(dy), z, core[dk]) for dy, dk in plane]
    for peer in peers:
        pl.semaphore_signal(barrier, inc=1, device_id=peer, device_id_type=MESH)
    unpack_w(0)
    unpack_w(1)
    pl.semaphore_wait(barrier, len(peers))

    yup, ydown = dev(c, yo(1), z, k), dev(c, yo(3), z, k)
    zup, zdown = dev(c, y, zo(1), k), dev(c, y, zo(NZ - 1), k)
    xup, xdown = dev(xo(1), y, z, k), dev(xo(3), y, z, k)
    for i in (1, 2, 3):
        send(g_ref, gall.at[c], gs.at[i - 1], gr.at[NX - i - 1], dev(xo(i), y, z, k))
    for n, (dy, dk) in enumerate(plane):
        rel = ((NY - dy) % NY) * 2 + dk
        send(cnt, cntall.at[rel], cs.at[n], cr.at[rel - 1], dev(c, yo(dy), z, core[dk]))
    cuts = (pl.ds(0, 48), pl.ds(48, 48), pl.ds(96, 48), pl.ds(144, 32))

    def send_wkv(s):
        for way, to in ((0, yup), (1, ydown)):
            off = way * 512 + s * PIECE
            send(
                wkvo.at[pl.ds(0, 2), pl.ds(pl.multiple_of(zp * 1024 + off, PIECE), PIECE), :],
                wkvx.at[zp, pl.ds(0, 2), pl.ds(off, PIECE), :],
                wys.at[way * SUBS + s], wyr.at[way * SUBS + s], to,
            )

    def send_x(i):
        send(x_ref.at[cuts[i], :], xall.at[c, k, cuts[i], :], xs.at[i], xr.at[i], xup)
        i = 3 - i
        send(x_ref.at[cuts[i], :], xall.at[c, k, cuts[i], :], xs.at[4 + i], xr.at[4 + i], xdown)

    left, right, far = xo(3), xo(1), xo(2)

    def relay_x(i):
        part = xall.at[left, k, cuts[i], :]
        landed(part, xr.at[i])
        send(part, part, xs.at[8 + i], xr.at[8 + i], xup)
        i = 3 - i
        part = xall.at[right, k, cuts[i], :]
        landed(part, xr.at[4 + i])
        send(part, part, xs.at[8 + i], xr.at[8 + i], xdown)

    send_x(0)
    unpack_w(2)
    unpack_w(3)
    send_wkv(0)
    send_x(1)
    unpack_w(4)
    unpack_w(5)
    send_wkv(1)
    send_x(2)
    send_x(3)
    send(x_ref, xall.at[c, k], ps.at[0], pr.at[0], partner)

    def send_wq(s):
        for way, to in ((0, yup), (1, ydown)):
            rows = pl.ds(way * 1024 + s * QPIECE, QPIECE)
            n = way * QSUBS + s
            send(wqo.at[rows, :], wqx.at[rows, :], wqs.at[n], wqr.at[n], to)

    for n in range(6, 16):
        unpack_w(n)

    row = lax.broadcasted_iota(jnp.int32, (2 * ROWS, 128), 0)
    lanes = lax.broadcasted_iota(jnp.int32, (2 * ROWS, 128), 1)
    place = (z * 8 + yh * 4 + r) * ROWS + row + jnp.where(row >= ROWS, ROWS, 0)
    angle = place.astype(F32) * inv_ref[...]
    cosb[...] = jnp.cos(angle)
    sine = jnp.sin(angle)
    sinb[...] = jnp.where(lanes < 64, -sine, sine)

    for n in range(7):
        landed(cntall.at[n + 1], cr.at[n])
    total = cntall[0]
    for n in range(7):
        total = total + cntall[n + 1]
    lane8 = lax.broadcasted_iota(jnp.int32, (8, 128), 1)
    bnd[z] = jnp.where((sub == 1) & (lane8 >= 3), BIG, total)

    def forward_w(s):
        for way, to in ((0, zup), (1, zdown)):
            rows = pl.ds(way * 512 + s * PIECE, PIECE)
            piece = wkvx.at[zp, pl.ds(0, 2), rows, :]
            landed(piece, wyr.at[way * SUBS + s])
            send(piece, piece, wzs.at[way * SUBS + s], wzr.at[way * SUBS + s], to)

    def bounds_hop(d):
        if d > 0:
            landed(bnd.at[zo(NZ - d)], br.at[2 * (d - 1)])
            if d < 4:
                landed(bnd.at[zo(d)], br.at[2 * (d - 1) + 1])
        if d < 4:
            send(bnd.at[zo(NZ - d)], bnd.at[zo(NZ - d)], bs.at[2 * d], br.at[2 * d], zup)
        if d < 3:
            send(bnd.at[zo(d)], bnd.at[zo(d)], bs.at[2 * d + 1], br.at[2 * d + 1], zdown)

    forward_w(0)
    send_wkv(2)
    bounds_hop(0)
    relay_x(0)
    relay_x(1)
    forward_w(1)
    send_wkv(3)
    bounds_hop(1)
    for i in (2, 3):
        landed(xall.at[left, k, cuts[i], :], xr.at[i])
        landed(xall.at[right, k, cuts[3 - i], :], xr.at[7 - i])
    send(xall.at[left, k], xall.at[left, k], ps.at[1], pr.at[1], partner)
    send(xall.at[right, k], xall.at[right, k], ps.at[2], pr.at[2], partner)
    forward_w(2)
    send_wq(0)
    bounds_hop(2)
    for i in range(4):
        landed(xall.at[far, k, cuts[i], :], xr.at[8 + i])
    send(xall.at[far, k], xall.at[far, k], ps.at[3], pr.at[3], partner)
    own_x.wait()
    own_g.wait()
    for i in (1, 2, 3):
        landed(gall.at[xo(i)], gr.at[i - 1])

    def normalise(kk, at):
        squares = jnp.zeros((ROWS, 128), F32)
        for cc in range(NX):
            for s in range(8):
                v = xall[cc, kk, :, s * 128 : (s + 1) * 128].astype(F32)
                squares = squares + v * v
        mean = jnp.sum(squares, axis=1, keepdims=True) * (1.0 / (NX * WIDTH))
        inverse = jnp.broadcast_to(lax.rsqrt(mean + 1e-05), (ROWS, 128))
        for cc in range(NX):
            for s in range(8):
                v = xall[cc, kk, :, s * 128 : (s + 1) * 128].astype(F32)
                gain = gall[cc, s : s + 1, :].astype(F32)
                xn[cc, at, s * 128 : (s + 1) * 128] = (v * inverse * gain).astype(BF16)

    normalise(k, pl.ds(pl.multiple_of(k * ROWS, ROWS), ROWS))
    forward_w(3)
    send_wq(1)
    bounds_hop(3)
    for n, block in enumerate((c, left, right, far)):
        landed(xall.at[block, 1 - k], pr.at[n])
    normalise(1 - k, pl.ds(pl.multiple_of((1 - k) * ROWS, ROWS), ROWS))
    for hh in range(2):
        out = slice(hh * 256, (hh + 1) * 256)
        acc[:, out] = jnp.dot(xn[2 * r], wkvo[hh, 0:1024], preferred_element_type=F32)
        acc[:, out] += jnp.dot(xn[2 * r + 1], wkvo[hh, 1024:2048], preferred_element_type=F32)
        acc[:, out] += jnp.dot(xn[2 * (1 - r) + zp], wkvx[zp, hh], preferred_element_type=F32)
    bounds_hop(4)
    for s in range(SUBS):
        for way in range(2):
            landed(
                wkvx.at[1 - zp, pl.ds(0, 2), pl.ds(way * 512 + s * PIECE, PIECE), :],
                wzr.at[way * SUBS + s],
            )
    for hh in range(2):
        out = slice(hh * 256, (hh + 1) * 256)
        acc[:, out] += jnp.dot(xn[2 * (1 - r) + 1 - zp], wkvx[1 - zp, hh], preferred_element_type=F32)

    def kv_at(p, zz, yy):
        return kv.at[p, zz, lax.div(yy, 2), pl.ds(0, 2), lax.rem(yy, 2)]

    for hh in range(2):
        u = acc[:, hh * 256 : hh * 256 + 128]
        u = u * cosb[...] + pltpu.roll(u, 64, 1) * sinb[...]
        stg[hh, 0, 0] = u[:ROWS].astype(BF16)
        stg[hh, 0, 1] = u[ROWS:].astype(BF16)
        u = acc[:, hh * 256 + 128 : hh * 256 + 256]
        stg[hh, 1, 0] = u[:ROWS].astype(BF16)
        stg[hh, 1, 1] = u[ROWS:].astype(BF16)
    exchange = []

    def exchange_send(source, slot_of, ssems, rsems):
        for hh in range(2):
            yd = 2 * k + hh
            rel = lax.rem(y - yd + NY, NY)
            for j in range(2):
                here = jnp.logical_and(yd == y, k == j)
                to = dev(c, yd, z, j)
                move = (source.at[hh, j], slot_of(j), ssems.at[hh * 2 + j], rsems.at[rel])

                @pl.when(here)
                def _():
                    pltpu.make_async_copy(move[0], move[1], move[3]).start()

                @pl.when(jnp.logical_not(here))
                def _():
                    pltpu.make_async_remote_copy(
                        src_ref=move[0], dst_ref=move[1], send_sem=move[2], recv_sem=move[3],
                        device_id=to, device_id_type=MESH,
                    ).start()

                exchange.append((here, move, to))

    exchange_send(stg, lambda j: kv_at(j, z, y), as_, akr)
    send_wq(2)
    send_wq(3)

    accq[...] = jnp.dot(xn[2 * r], wqo[0:1024, :], preferred_element_type=F32)
    accq[...] += jnp.dot(xn[2 * r + 1], wqo[1024:2048, :], preferred_element_type=F32)

    def project_q(part):
        for s in (2 * part, 2 * part + 1):
            for way in range(2):
                landed(
                    wqx.at[pl.ds(way * 1024 + s * QPIECE, QPIECE), :], wqr.at[way * QSUBS + s]
                )
        low = part * 512
        for way in range(2):
            accq[...] += jnp.dot(
                xn[2 * (1 - r) + way, :, low : low + 512],
                wqx[way * 1024 + low : way * 1024 + low + 512, :],
                preferred_element_type=F32,
            )

    project_q(0)
    for u in ORDER:
        block = kv_at(k, z, yo(u))
        landed(block, akr.at[u])
        send(block, block, rs.at[u], rp.at[u], zup)
        send(block, block, rs.at[4 + u], rm.at[u], zdown)
        send(block, block, pks.at[u], pkr.at[u], partner)

    def ring(d, pieces):
        up, down = zo(NZ - d), zo(d)
        for u in pieces:
            if d < 4 or u in PLUS:
                block = kv_at(k, up, yo(u))
                landed(block, rp.at[(d - 1) * 4 + u])
                if d < 3 or (d == 3 and u in PLUS):
                    send(block, block, rs.at[d * 8 + u], rp.at[d * 4 + u], zup)
                n = (2 * d - 1) * 4 + u
                send(block, block, pks.at[n], pkr.at[n], partner)
            if d < 4 or u in MINUS:
                block = kv_at(k, down, yo(u))
                landed(block, rm.at[(d - 1) * 4 + u])
                if d < 3 or (d == 3 and u in MINUS):
                    send(block, block, rs.at[d * 8 + 4 + u], rm.at[d * 4 + u], zdown)
                n = (2 * d if d < 4 else 7) * 4 + u
                send(block, block, pks.at[n], pkr.at[n], partner)
    project_q(1)
    for hh in range(2):
        u = accq[:, hh * 128 : (hh + 1) * 128]
        u = u * cosb[...] + pltpu.roll(u, 64, 1) * sinb[...]
        stgq[hh, 0] = u[:ROWS].astype(BF16)
        stgq[hh, 1] = u[ROWS:].astype(BF16)
    exchange_send(stgq, lambda j: qb.at[y], aqs, aqr)

    ring(1, ORDER)

    mrun[...] = jnp.full_like(mrun, HIDE)
    oacc[...] = jnp.zeros_like(oacc)
    qrow = lax.broadcasted_iota(jnp.int32, (4 * ROWS, 128), 0)
    qplace = (qrow + jnp.where(qrow >= 2 * ROWS, 2 * ROWS, 0) + 2 * ROWS * k).astype(F32)
    mine = bnd[z]
    inside = (qplace >= mine[0:1, :]) & (qplace < mine[1:2, :])
    qcat[:, 128:256] = jnp.where(inside, 1.0, 0.0).astype(BF16)
    for u in ORDER:
        landed(qb.at[yo(u)], aqr.at[u])
    for n in range(4):
        qcat[n * ROWS : (n + 1) * ROWS, 0:128] = qb[n]

    def attend(zz, diagonal):
        limit = bnd[zz]
        krow = lax.broadcasted_iota(jnp.int32, (8 * ROWS, 128), 0).astype(F32)
        kin = (krow >= limit[0:1, :]) & (krow < limit[1:2, :])
        kaug[...] = jnp.where(kin, 0.0, HIDE).astype(BF16)

        keys = jnp.concatenate([kv[0, zz].reshape(8 * ROWS, 128), kaug[...]], axis=1)
        values = kv[1, zz].reshape(8 * ROWS, 128)
        values = jnp.concatenate([values, jnp.ones_like(values)], axis=1)

        def scored(i):
            rows = slice(i * 2 * ROWS, (i + 1) * 2 * ROWS)
            return lax.dot_general(
                qcat[rows, :], keys, (((1,), (1,)), ((), ())), preferred_element_type=F32
            )

        def absorb(i, scores):
            rows = slice(i * 2 * ROWS, (i + 1) * 2 * ROWS)
            if diagonal:
                shape = (2 * ROWS, 8 * ROWS)
                qp = lax.broadcasted_iota(jnp.int32, shape, 0) + i * 4 * ROWS + 2 * ROWS * k
                kp = lax.broadcasted_iota(jnp.int32, shape, 1)
                scores = jnp.where(kp <= qp, scores, HIDE)
            before = mrun[rows, :]
            newest = jnp.maximum(before, jnp.max(scores, axis=1, keepdims=True))
            weights = jnp.exp2((scores - newest[:, 0:1]) * SCALE).astype(BF16)
            factor = jnp.exp2((before - newest) * SCALE)
            added = jnp.dot(weights, values, preferred_element_type=F32)
            oacc[rows, :] = oacc[rows, :] * jnp.concatenate([factor, factor], axis=1) + added
            mrun[rows, :] = newest

        first = scored(0)
        second = scored(1)
        absorb(0, first)
        absorb(1, second)

    def shared(zz, n):
        for u in ORDER:
            landed(kv_at(1 - k, zz, yo(u)), pkr.at[n * 4 + u])

    def attend_up(d):
        shared(zo(NZ - d), 2 * d - 1)

        @pl.when(z >= d)
        def _():
            attend(zo(NZ - d), False)

    def attend_down(d):
        shared(zo(d), 2 * d)

        @pl.when(z + d >= NZ)
        def _():
            attend(zo(d), False)

    shared(z, 0)
    attend(z, True)
    ring(2, ORDER)
    attend_up(1)
    attend_down(1)
    ring(3, ORDER[:2])
    attend_up(2)
    ring(3, ORDER[2:])
    attend_down(2)
    ring(4, ORDER)
    attend_up(3)
    attend_down(3)
    attend_up(4)

    result = (oacc[:, 0:128] / oacc[:, 128:256]).astype(BF16)
    for n in range(4):
        osend[n] = result[n * ROWS : (n + 1) * ROWS]
    obuf[y] = osend[y]
    for dy in (1, 2, 3):
        send(osend.at[yo(dy)], obuf.at[y], os_.at[dy - 1], orr.at[NY - dy - 1], dev(c, yo(dy), z, k))
    for dy in (1, 2, 3):
        landed(obuf.at[yo(dy)], orr.at[dy - 1])
    for h in range(4):
        o_ref[:, h * 128 : (h + 1) * 128] = obuf[h]

    for here, move, to in exchange:

        @pl.when(jnp.logical_not(here))
        def _():
            pltpu.make_async_remote_copy(
                src_ref=move[0], dst_ref=move[1], send_sem=move[2], recv_sem=move[3],
                device_id=to, device_id_type=MESH,
            ).wait_send()

    for copy in pending:
        copy.wait_send()


def per_device(activations, norm_gain, qkv_weight, doc_ids):
    spacing = np.arange(64).astype(np.float32) * np.float32(2.0 / 128)
    inverse = np.power(np.float32(10000.0), -spacing).astype(np.float32)
    inverse = np.concatenate([inverse, inverse])[None, :]
    dma = pltpu.SemaphoreType.DMA
    anywhere = pl.BlockSpec(memory_space=pl.ANY)
    local = pl.BlockSpec(memory_space=pltpu.VMEM)
    scratch = [
        pltpu.VMEM((NX, 2, ROWS, WIDTH), BF16),
        pltpu.VMEM((NX, 8, 128), BF16),
        pltpu.VMEM((HALF, 4, 384), BF16),
        pltpu.VMEM((2, HALF, 256), BF16),
        pltpu.VMEM((2, 2, 1024, 256), BF16),
        pltpu.VMEM((HALF, 256), BF16),
        pltpu.VMEM((HALF, 256), BF16),
        pltpu.VMEM((8, 128), F32),
        pltpu.VMEM((8, 8, 128), F32),
        pltpu.VMEM((NZ, 8, 128), F32),
        pltpu.VMEM((NX, 2 * ROWS, WIDTH), BF16),
        pltpu.VMEM((2 * ROWS, 512), F32),
        pltpu.VMEM((2 * ROWS, 256), F32),
        pltpu.VMEM((2 * ROWS, 128), F32),
        pltpu.VMEM((2 * ROWS, 128), F32),
        pltpu.VMEM((2, 2, 2, ROWS, 128), BF16),
        pltpu.VMEM((2, 2, ROWS, 128), BF16),
        pltpu.VMEM((2, NZ, 2, 2, 2, ROWS, 128), BF16),
        pltpu.VMEM((NY, ROWS, 128), BF16),
        pltpu.VMEM((4 * ROWS, 256), BF16),
        pltpu.VMEM((8 * ROWS, 128), BF16),
        pltpu.VMEM((4 * ROWS, 128), F32),
        pltpu.VMEM((4 * ROWS, 256), F32),
        pltpu.VMEM((NY, ROWS, 128), BF16),
        pltpu.VMEM((NY, ROWS, 128), BF16),
        dma((18,)),
        dma((2 * SUBS,)), dma((2 * SUBS,)),
        dma((2 * SUBS,)), dma((2 * SUBS,)),
        dma((2 * QSUBS,)), dma((2 * QSUBS,)),
        dma((12,)), dma((12,)),
        dma((3,)), dma((3,)),
        dma((4,)), dma((4,)),
        dma((7,)), dma((7,)),
        dma((8,)), dma((8,)),
        dma((4,)), dma((4,)), dma((4,)), dma((4,)),
        dma((32,)), dma((16,)), dma((16,)),
        dma((32,)), dma((32,)),
        dma((3,)), dma((3,)),
    ]
    return pl.pallas_call(
        kernel,
        out_shape=jax.ShapeDtypeStruct((ROWS, 512), BF16),
        in_specs=[anywhere, anywhere, anywhere, local, local],
        out_specs=local,
        scratch_shapes=scratch,
        compiler_params=pltpu.CompilerParams(
            collective_id=0, has_side_effects=True, vmem_limit_bytes=60 * 1024 * 1024
        ),
        name="attention_block",
    )(
        activations, norm_gain.reshape(8, 128), qkv_weight, doc_ids.reshape(1, ROWS), jnp.asarray(inverse)
    )


def solution(mesh):
    placed = (P(("tok", "row"), "col"), P("col"), P("row", "col", None), P(("tok", "row")))
    return jax.shard_map(
        per_device, mesh=mesh, in_specs=placed, out_specs=P(("tok", "row"), "col"), check_vma=False
    )
```

```python
import functools
import math

import jax
import jax.numpy as jnp
import numpy as np
from jax import lax
from jax.experimental import pallas as pl
from jax.experimental.pallas import tpu as pltpu
from jax.sharding import PartitionSpec as P

MESH = pl.DeviceIdType.MESH
F32 = jnp.float32
BF16 = jnp.bfloat16
NX, NY, NZ = 4, 4, 8
ROWS = 176
WIDTH = 1024
HALF = 2048
SUBS = 8
PIECE = 512 // SUBS
QSUBS = 4
QPIECE = 1024 // QSUBS
HIDE = -1e30
BIG = 1e9
PLUS = (0, 1)
MINUS = (3, 2)
ORDER = (0, 1, 3, 2)
SCALE = math.log2(math.e) / math.sqrt(128.0)


def kernel(
    x_ref, g_ref, w_ref, doc_ref, inv_ref, o_ref,
    xall, gall, raw, wkvo, wkvx, wqo, wqx, cnt, cntall, bnd, xn, acc, accq, cosb, sinb, stg, stgq, kv, qb, qcat, kaug,
    mrun, oacc, osend, obuf,
    lsem, wys, wyr, wzs, wzr, wqs, wqr, xs, xr, gs, gr, ps, pr, cs, cr, bs, br, as_, akr, aqs, aqr,
    rs, rp, rm, pks, pkr, os_, orr,
):
    t = lax.axis_index("tok")
    r = lax.axis_index("row")
    c = lax.axis_index("col")
    k = lax.rem(t, 2)
    yh = lax.rem(lax.div(t, 2), 2)
    z = lax.div(t, 4)
    y = yh * 2 + r
    zp = lax.rem(z, 2)

    def dev(cx, cy, cz, ck):
        return ((cz * 2 + lax.div(cy, 2)) * 2 + ck, lax.rem(cy, 2), cx)

    def xo(i):
        return lax.rem(c + i, NX)

    def yo(i):
        return lax.rem(y + i, NY)

    def zo(i):
        return lax.rem(z + i, NZ)

    partner = dev(c, y, z, 1 - k)
    pending = []

    def send(src, dst, ssem, rsem, to):
        copy = pltpu.make_async_remote_copy(
            src_ref=src, dst_ref=dst, send_sem=ssem, recv_sem=rsem,
            device_id=to, device_id_type=MESH,
        )
        copy.start()
        pending.append(copy)

    def landed(dst, rsem):
        pltpu.make_async_copy(dst, dst, rsem).wait()

    own_x = pltpu.make_async_copy(x_ref, xall.at[c, k], lsem.at[0])
    own_g = pltpu.make_async_copy(g_ref, gall.at[c], lsem.at[1])
    def raw_rows(n):
        half = zp if n < 8 else 1 - zp
        off = (n % 2) * 512 + (n % 8) // 2 * 128
        return pl.ds(pl.multiple_of(half * 1024 + off, 128), 128)

    raw_copies = [
        pltpu.make_async_copy(w_ref.at[raw_rows(n)], raw.at[raw_rows(n)], lsem.at[2 + n])
        for n in range(16)
    ]
    for copy in raw_copies:
        copy.start()
    own_x.start()
    own_g.start()

    def unpack_w(n):
        raw_copies[n].wait()
        rows = raw_rows(n)
        heads = jnp.swapaxes(raw[rows], 0, 1)
        for hh in range(2):
            head = jnp.where(k == 0, heads[hh], heads[2 + hh])
            wqo[rows, hh * 128 : (hh + 1) * 128] = head[:, 0:128]
            wkvo[hh, rows, :] = head[:, 128:384]


    lane = lax.broadcasted_iota(jnp.int32, (1, 128), 1)
    ids = doc_ref[...]
    below = [jnp.sum((ids < d).astype(F32), axis=1, keepdims=True) for d in (1, 2, 3)]
    low = sum(jnp.where(lane == d + 1, below[d], 0.0) for d in range(3))
    high = sum(jnp.where(lane == d, below[d], 0.0) for d in range(3))
    sub = lax.broadcasted_iota(jnp.int32, (8, 128), 0)
    counts = jnp.where(sub == 0, low, jnp.where(sub == 1, high, 0.0))
    cnt[...] = counts
    cntall[0] = counts

    barrier = pltpu.get_barrier_semaphore()
    peers = [dev(xo(i), y, z, k) for i in (1, 2, 3)]
    peers += [dev(c, y, zo(1), k), dev(c, y, zo(NZ - 1), k)]
    plane = [(dy, dk) for dy in range(NY) for dk in range(2) if (dy, dk) != (0, 0)]
    core = (k, 1 - k)
    peers += [dev(c, yo(dy), z, core[dk]) for dy, dk in plane]
    for peer in peers:
        pl.semaphore_signal(barrier, inc=1, device_id=peer, device_id_type=MESH)
    unpack_w(0)
    unpack_w(1)
    pl.semaphore_wait(barrier, len(peers))

    yup, ydown = dev(c, yo(1), z, k), dev(c, yo(3), z, k)
    zup, zdown = dev(c, y, zo(1), k), dev(c, y, zo(NZ - 1), k)
    xup, xdown = dev(xo(1), y, z, k), dev(xo(3), y, z, k)
    for i in (1, 2, 3):
        send(g_ref, gall.at[c], gs.at[i - 1], gr.at[NX - i - 1], dev(xo(i), y, z, k))
    for n, (dy, dk) in enumerate(plane):
        rel = ((NY - dy) % NY) * 2 + dk
        send(cnt, cntall.at[rel], cs.at[n], cr.at[rel - 1], dev(c, yo(dy), z, core[dk]))
    cuts = (pl.ds(0, 48), pl.ds(48, 48), pl.ds(96, 48), pl.ds(144, 32))

    def send_wkv(s):
        for way, to in ((0, yup), (1, ydown)):
            off = way * 512 + s * PIECE
            send(
                wkvo.at[pl.ds(0, 2), pl.ds(pl.multiple_of(zp * 1024 + off, PIECE), PIECE), :],
                wkvx.at[zp, pl.ds(0, 2), pl.ds(off, PIECE), :],
                wys.at[way * SUBS + s], wyr.at[way * SUBS + s], to,
            )

    def send_x(i):
        send(x_ref.at[cuts[i], :], xall.at[c, k, cuts[i], :], xs.at[i], xr.at[i], xup)
        i = 3 - i
        send(x_ref.at[cuts[i], :], xall.at[c, k, cuts[i], :], xs.at[4 + i], xr.at[4 + i], xdown)

    left, right, far = xo(3), xo(1), xo(2)

    def relay_x(i):
        part = xall.at[left, k, cuts[i], :]
        landed(part, xr.at[i])
        send(part, part, xs.at[8 + i], xr.at[8 + i], xup)
        i = 3 - i
        part = xall.at[right, k, cuts[i], :]
        landed(part, xr.at[4 + i])
        send(part, part, xs.at[8 + i], xr.at[8 + i], xdown)

    send_wkv(0)
    send_x(0)
    send_wkv(1)
    unpack_w(2)
    unpack_w(3)
    send_x(1)
    unpack_w(4)
    unpack_w(5)
    send_wkv(2)
    send_wkv(3)

    def send_wq(s):
        for way, to in ((0, yup), (1, ydown)):
            rows = pl.ds(way * 1024 + s * QPIECE, QPIECE)
            n = way * QSUBS + s
            send(wqo.at[rows, :], wqx.at[rows, :], wqs.at[n], wqr.at[n], to)

    for n in range(6, 16):
        unpack_w(n)

    row = lax.broadcasted_iota(jnp.int32, (2 * ROWS, 128), 0)
    lanes = lax.broadcasted_iota(jnp.int32, (2 * ROWS, 128), 1)
    place = (z * 8 + yh * 4 + r) * ROWS + row + jnp.where(row >= ROWS, ROWS, 0)
    angle = place.astype(F32) * inv_ref[...]
    cosb[...] = jnp.cos(angle)
    sine = jnp.sin(angle)
    sinb[...] = jnp.where(lanes < 64, -sine, sine)

    for n in range(7):
        landed(cntall.at[n + 1], cr.at[n])
    total = cntall[0]
    for n in range(7):
        total = total + cntall[n + 1]
    lane8 = lax.broadcasted_iota(jnp.int32, (8, 128), 1)
    bnd[z] = jnp.where((sub == 1) & (lane8 >= 3), BIG, total)

    def forward_w(s):
        for way, to in ((0, zup), (1, zdown)):
            rows = pl.ds(way * 512 + s * PIECE, PIECE)
            piece = wkvx.at[zp, pl.ds(0, 2), rows, :]
            landed(piece, wyr.at[way * SUBS + s])
            send(piece, piece, wzs.at[way * SUBS + s], wzr.at[way * SUBS + s], to)

    def bounds_hop(d):
        if d > 0:
            landed(bnd.at[zo(NZ - d)], br.at[2 * (d - 1)])
            if d < 4:
                landed(bnd.at[zo(d)], br.at[2 * (d - 1) + 1])
        if d < 4:
            send(bnd.at[zo(NZ - d)], bnd.at[zo(NZ - d)], bs.at[2 * d], br.at[2 * d], zup)
        if d < 3:
            send(bnd.at[zo(d)], bnd.at[zo(d)], bs.at[2 * d + 1], br.at[2 * d + 1], zdown)

    send_x(2)
    forward_w(0)
    send_wkv(4)
    forward_w(1)
    send_wkv(5)
    send_x(3)
    bounds_hop(0)
    relay_x(0)
    relay_x(1)
    send(x_ref, xall.at[c, k], ps.at[0], pr.at[0], partner)
    forward_w(2)
    send_wkv(6)
    forward_w(3)
    send_wkv(7)
    bounds_hop(1)
    for i in (2, 3):
        landed(xall.at[left, k, cuts[i], :], xr.at[i])
        landed(xall.at[right, k, cuts[3 - i], :], xr.at[7 - i])
    send(xall.at[left, k], xall.at[left, k], ps.at[1], pr.at[1], partner)
    send(xall.at[right, k], xall.at[right, k], ps.at[2], pr.at[2], partner)
    forward_w(4)
    send_wq(0)
    forward_w(5)
    bounds_hop(2)
    for i in range(4):
        landed(xall.at[far, k, cuts[i], :], xr.at[8 + i])
    send(xall.at[far, k], xall.at[far, k], ps.at[3], pr.at[3], partner)
    forward_w(6)
    own_x.wait()
    own_g.wait()
    for i in (1, 2, 3):
        landed(gall.at[xo(i)], gr.at[i - 1])

    def normalise(kk, at):
        squares = jnp.zeros((ROWS, 128), F32)
        for cc in range(NX):
            for s in range(8):
                v = xall[cc, kk, :, s * 128 : (s + 1) * 128].astype(F32)
                squares = squares + v * v
        mean = jnp.sum(squares, axis=1, keepdims=True) * (1.0 / (NX * WIDTH))
        inverse = jnp.broadcast_to(lax.rsqrt(mean + 1e-05), (ROWS, 128))
        for cc in range(NX):
            for s in range(8):
                v = xall[cc, kk, :, s * 128 : (s + 1) * 128].astype(F32)
                gain = gall[cc, s : s + 1, :].astype(F32)
                xn[cc, at, s * 128 : (s + 1) * 128] = (v * inverse * gain).astype(BF16)

    normalise(k, pl.ds(pl.multiple_of(k * ROWS, ROWS), ROWS))
    forward_w(7)
    send_wq(1)
    for n, block in enumerate((c, left, right, far)):
        landed(xall.at[block, 1 - k], pr.at[n])
    normalise(1 - k, pl.ds(pl.multiple_of((1 - k) * ROWS, ROWS), ROWS))
    for hh in range(2):
        out = slice(hh * 256, (hh + 1) * 256)
        acc[:, out] = jnp.dot(xn[2 * r], wkvo[hh, 0:1024], preferred_element_type=F32)
        acc[:, out] += jnp.dot(xn[2 * r + 1], wkvo[hh, 1024:2048], preferred_element_type=F32)
    for hh in range(2):
        out = slice(hh * 256, (hh + 1) * 256)
        acc[:, out] += jnp.dot(xn[2 * (1 - r) + zp], wkvx[zp, hh], preferred_element_type=F32)
    for s in range(SUBS):
        for way in range(2):
            landed(
                wkvx.at[1 - zp, pl.ds(0, 2), pl.ds(way * 512 + s * PIECE, PIECE), :],
                wzr.at[way * SUBS + s],
            )
    for hh in range(2):
        out = slice(hh * 256, (hh + 1) * 256)
        acc[:, out] += jnp.dot(xn[2 * (1 - r) + 1 - zp], wkvx[1 - zp, hh], preferred_element_type=F32)

    def kv_at(p, zz, yy):
        return kv.at[p, zz, lax.div(yy, 2), pl.ds(0, 2), lax.rem(yy, 2)]

    for hh in range(2):
        u = acc[:, hh * 256 : hh * 256 + 128]
        u = u * cosb[...] + pltpu.roll(u, 64, 1) * sinb[...]
        stg[hh, 0, 0] = u[:ROWS].astype(BF16)
        stg[hh, 0, 1] = u[ROWS:].astype(BF16)
        u = acc[:, hh * 256 + 128 : hh * 256 + 256]
        stg[hh, 1, 0] = u[:ROWS].astype(BF16)
        stg[hh, 1, 1] = u[ROWS:].astype(BF16)
    exchange = []

    def exchange_send(source, slot_of, ssems, rsems):
        for step in range(2):
            hh = step
            yd = 2 * k + hh
            rel = lax.rem(y - yd + NY, NY)
            for j in range(2):
                here = jnp.logical_and(yd == y, k == j)
                to = dev(c, yd, z, j)
                move = (source.at[hh, j], slot_of(j), ssems.at[hh * 2 + j], rsems.at[rel])

                @pl.when(here)
                def _():
                    pltpu.make_async_copy(move[0], move[1], move[3]).start()

                @pl.when(jnp.logical_not(here))
                def _():
                    pltpu.make_async_remote_copy(
                        src_ref=move[0], dst_ref=move[1], send_sem=move[2], recv_sem=move[3],
                        device_id=to, device_id_type=MESH,
                    ).start()

                exchange.append((here, move, to))

    exchange_send(stg, lambda j: kv_at(j, z, y), as_, akr)
    send_wq(2)
    send_wq(3)

    def ring_start(u):
        block = kv_at(k, z, yo(u))
        landed(block, akr.at[u])
        send(block, block, rs.at[u], rp.at[u], zup)
        send(block, block, rs.at[4 + u], rm.at[u], zdown)
        send(block, block, pks.at[u], pkr.at[u], partner)

    ring_start(0)
    accq[...] = jnp.dot(xn[2 * r], wqo[0:1024, :], preferred_element_type=F32)
    accq[...] += jnp.dot(xn[2 * r + 1], wqo[1024:2048, :], preferred_element_type=F32)

    def project_q(part):
        for s in (2 * part, 2 * part + 1):
            for way in range(2):
                landed(
                    wqx.at[pl.ds(way * 1024 + s * QPIECE, QPIECE), :], wqr.at[way * QSUBS + s]
                )
        low = part * 512
        for way in range(2):
            accq[...] += jnp.dot(
                xn[2 * (1 - r) + way, :, low : low + 512],
                wqx[way * 1024 + low : way * 1024 + low + 512, :],
                preferred_element_type=F32,
            )


    def ring(d, pieces):
        up, down = zo(NZ - d), zo(d)
        for u in pieces:
            if d < 4 or u in PLUS:
                block = kv_at(k, up, yo(u))
                landed(block, rp.at[(d - 1) * 4 + u])
                if d < 3 or (d == 3 and u in PLUS):
                    send(block, block, rs.at[d * 8 + u], rp.at[d * 4 + u], zup)
                n = (2 * d - 1) * 4 + u
                send(block, block, pks.at[n], pkr.at[n], partner)
            if d < 4 or u in MINUS:
                block = kv_at(k, down, yo(u))
                landed(block, rm.at[(d - 1) * 4 + u])
                if d < 3 or (d == 3 and u in MINUS):
                    send(block, block, rs.at[d * 8 + 4 + u], rm.at[d * 4 + u], zdown)
                n = (2 * d if d < 4 else 7) * 4 + u
                send(block, block, pks.at[n], pkr.at[n], partner)
    ring(1, (0,))
    ring_start(1)
    ring_start(3)
    ring_start(2)
    bounds_hop(3)
    project_q(0)
    ring(2, (0,))
    project_q(1)
    for hh in range(2):
        u = accq[:, hh * 128 : (hh + 1) * 128]
        u = u * cosb[...] + pltpu.roll(u, 64, 1) * sinb[...]
        stgq[hh, 0] = u[:ROWS].astype(BF16)
        stgq[hh, 1] = u[ROWS:].astype(BF16)
    exchange_send(stgq, lambda j: qb.at[y], aqs, aqr)

    ring(1, (1, 3, 2))
    bounds_hop(4)

    mrun[...] = jnp.full_like(mrun, HIDE)
    oacc[...] = jnp.zeros_like(oacc)
    qrow = lax.broadcasted_iota(jnp.int32, (4 * ROWS, 128), 0)
    qplace = (qrow + jnp.where(qrow >= 2 * ROWS, 2 * ROWS, 0) + 2 * ROWS * k).astype(F32)
    mine = bnd[z]
    inside = (qplace >= mine[0:1, :]) & (qplace < mine[1:2, :])
    qcat[:, 128:256] = jnp.where(inside, 1.0, 0.0).astype(BF16)
    for u in ORDER:
        landed(qb.at[yo(u)], aqr.at[u])
    for n in range(4):
        qcat[n * ROWS : (n + 1) * ROWS, 0:128] = qb[n]

    def out_copy(yq):
        return pltpu.make_async_remote_copy(
            src_ref=osend.at[yq], dst_ref=obuf.at[y], send_sem=os_.at[yq],
            recv_sem=orr.at[lax.rem(y - yq + NY, NY)],
            device_id=dev(c, yq, z, k), device_id_type=MESH,
        )

    def out_tile(i):
        rows = slice(i * 2 * ROWS, (i + 1) * 2 * ROWS)
        result = (oacc[rows, 0:128] / oacc[rows, 128:256]).astype(BF16)
        for n in range(2):
            osend[2 * i + n] = result[n * ROWS : (n + 1) * ROWS]
        for n in range(2):
            yq = 2 * i + n

            @pl.when(y == yq)
            def _():
                obuf[yq] = osend[yq]

            @pl.when(y != yq)
            def _():
                out_copy(yq).start()

    def attend(zz, diagonal, after=None):
        limit = bnd[zz]
        krow = lax.broadcasted_iota(jnp.int32, (8 * ROWS, 128), 0).astype(F32)
        kin = (krow >= limit[0:1, :]) & (krow < limit[1:2, :])
        kaug[...] = jnp.where(kin, 0.0, HIDE).astype(BF16)

        keys = jnp.concatenate([kv[0, zz].reshape(8 * ROWS, 128), kaug[...]], axis=1)
        values = kv[1, zz].reshape(8 * ROWS, 128)
        values = jnp.concatenate([values, jnp.ones_like(values)], axis=1)

        def scored(i):
            rows = slice(i * 2 * ROWS, (i + 1) * 2 * ROWS)
            return lax.dot_general(
                qcat[rows, :], keys, (((1,), (1,)), ((), ())), preferred_element_type=F32
            )

        def absorb(i, scores):
            rows = slice(i * 2 * ROWS, (i + 1) * 2 * ROWS)
            if diagonal:
                shape = (2 * ROWS, 8 * ROWS)
                qp = lax.broadcasted_iota(jnp.int32, shape, 0) + i * 4 * ROWS + 2 * ROWS * k
                kp = lax.broadcasted_iota(jnp.int32, shape, 1)
                scores = jnp.where(kp <= qp, scores, HIDE)
            before = mrun[rows, :]
            newest = jnp.maximum(before, jnp.max(scores, axis=1, keepdims=True))
            weights = jnp.exp2((scores - newest[:, 0:1]) * SCALE).astype(BF16)
            factor = jnp.exp2((before - newest) * SCALE)
            added = jnp.dot(weights, values, preferred_element_type=F32)
            oacc[rows, :] = oacc[rows, :] * jnp.concatenate([factor, factor], axis=1) + added
            mrun[rows, :] = newest

        first = scored(0)
        second = scored(1)
        for i, scores in enumerate((first, second)):
            absorb(i, scores)
            if after is not None:
                after(i)

    def shared(zz, n):
        for u in ORDER:
            landed(kv_at(1 - k, zz, yo(u)), pkr.at[n * 4 + u])

    def attend_up(d):
        shared(zo(NZ - d), 2 * d - 1)

        @pl.when(z >= d)
        def _():
            attend(zo(NZ - d), False)

    def attend_down(d):
        shared(zo(d), 2 * d)

        @pl.when(z + d >= NZ)
        def _():
            attend(zo(d), False)

    shared(z, 0)
    attend(z, True)
    ring(3, (0,))
    ring(2, (1,))
    attend_up(1)
    ring(2, (3, 2))
    attend_down(1)
    attend_up(2)
    ring(4, (0,))
    ring(3, (1,))
    attend_down(2)
    ring(3, (3, 2))
    attend_up(3)
    ring(4, (3,))
    attend_down(3)
    ring(4, (1, 2))
    shared(zo(4), 7)

    @pl.when(z >= 4)
    def _():
        attend(zo(4), False, out_tile)

    @pl.when(z < 4)
    def _():
        out_tile(0)
        out_tile(1)

    for dy in (1, 2, 3):
        landed(obuf.at[yo(dy)], orr.at[dy])
    for h in range(4):
        o_ref[:, h * 128 : (h + 1) * 128] = obuf[h]

    for here, move, to in exchange:

        @pl.when(jnp.logical_not(here))
        def _():
            pltpu.make_async_remote_copy(
                src_ref=move[0], dst_ref=move[1], send_sem=move[2], recv_sem=move[3],
                device_id=to, device_id_type=MESH,
            ).wait_send()

    for yq in range(NY):

        @pl.when(y != yq)
        def _():
            out_copy(yq).wait_send()

    for copy in pending:
        copy.wait_send()


def per_device(activations, norm_gain, qkv_weight, doc_ids):
    spacing = np.arange(64).astype(np.float32) * np.float32(2.0 / 128)
    inverse = np.power(np.float32(10000.0), -spacing).astype(np.float32)
    inverse = np.concatenate([inverse, inverse])[None, :]
    dma = pltpu.SemaphoreType.DMA
    anywhere = pl.BlockSpec(memory_space=pl.ANY)
    local = pl.BlockSpec(memory_space=pltpu.VMEM)
    scratch = [
        pltpu.VMEM((NX, 2, ROWS, WIDTH), BF16),
        pltpu.VMEM((NX, 8, 128), BF16),
        pltpu.VMEM((HALF, 4, 384), BF16),
        pltpu.VMEM((2, HALF, 256), BF16),
        pltpu.VMEM((2, 2, 1024, 256), BF16),
        pltpu.VMEM((HALF, 256), BF16),
        pltpu.VMEM((HALF, 256), BF16),
        pltpu.VMEM((8, 128), F32),
        pltpu.VMEM((8, 8, 128), F32),
        pltpu.VMEM((NZ, 8, 128), F32),
        pltpu.VMEM((NX, 2 * ROWS, WIDTH), BF16),
        pltpu.VMEM((2 * ROWS, 512), F32),
        pltpu.VMEM((2 * ROWS, 256), F32),
        pltpu.VMEM((2 * ROWS, 128), F32),
        pltpu.VMEM((2 * ROWS, 128), F32),
        pltpu.VMEM((2, 2, 2, ROWS, 128), BF16),
        pltpu.VMEM((2, 2, ROWS, 128), BF16),
        pltpu.VMEM((2, NZ, 2, 2, 2, ROWS, 128), BF16),
        pltpu.VMEM((NY, ROWS, 128), BF16),
        pltpu.VMEM((4 * ROWS, 256), BF16),
        pltpu.VMEM((8 * ROWS, 128), BF16),
        pltpu.VMEM((4 * ROWS, 128), F32),
        pltpu.VMEM((4 * ROWS, 256), F32),
        pltpu.VMEM((NY, ROWS, 128), BF16),
        pltpu.VMEM((NY, ROWS, 128), BF16),
        dma((18,)),
        dma((2 * SUBS,)), dma((2 * SUBS,)),
        dma((2 * SUBS,)), dma((2 * SUBS,)),
        dma((2 * QSUBS,)), dma((2 * QSUBS,)),
        dma((12,)), dma((12,)),
        dma((3,)), dma((3,)),
        dma((4,)), dma((4,)),
        dma((7,)), dma((7,)),
        dma((8,)), dma((8,)),
        dma((4,)), dma((4,)), dma((4,)), dma((4,)),
        dma((32,)), dma((16,)), dma((16,)),
        dma((32,)), dma((32,)),
        dma((4,)), dma((4,)),
    ]
    return pl.pallas_call(
        kernel,
        out_shape=jax.ShapeDtypeStruct((ROWS, 512), BF16),
        in_specs=[anywhere, anywhere, anywhere, local, local],
        out_specs=local,
        scratch_shapes=scratch,
        compiler_params=pltpu.CompilerParams(
            collective_id=0, has_side_effects=True, vmem_limit_bytes=60 * 1024 * 1024
        ),
        name="attention_block",
    )(
        activations, norm_gain.reshape(8, 128), qkv_weight, doc_ids.reshape(1, ROWS), jnp.asarray(inverse)
    )


def solution(mesh):
    placed = (P(("tok", "row"), "col"), P("col"), P("row", "col", None), P(("tok", "row")))
    return jax.shard_map(
        per_device, mesh=mesh, in_specs=placed, out_specs=P(("tok", "row"), "col"), check_vma=False
    )
```

```python
import functools
import math

import jax
import jax.numpy as jnp
import numpy as np
from jax import lax
from jax.experimental import pallas as pl
from jax.experimental.pallas import tpu as pltpu
from jax.sharding import PartitionSpec as P

MESH = pl.DeviceIdType.MESH
F32 = jnp.float32
BF16 = jnp.bfloat16
NX, NY, NZ = 4, 4, 8
ROWS = 176
WIDTH = 1024
HALF = 2048
SUBS = 8
PIECE = 512 // SUBS
QSUBS = 4
QPIECE = 1024 // QSUBS
HIDE = -1e30
BIG = 1e9
PLUS = (0, 1)
MINUS = (3, 2)
ORDER = (0, 1, 3, 2)
SCALE = math.log2(math.e) / math.sqrt(128.0)


def kernel(
    x_ref, g_ref, w_ref, doc_ref, inv_ref, o_ref,
    xall, gall, raw, wkvo, wkvx, wqo, wqx, cnt, cntall, bnd, xn, acc, accq, cosb, sinb, stg, stgq, kv, qb, qcat, kaug,
    mrun, oacc, osend, obuf,
    lsem, wys, wyr, wzs, wzr, wqs, wqr, xs, xr, gs, gr, ps, pr, cs, cr, bs, br, as_, akr, aqs, aqr,
    rs, rp, rm, pks, pkr, os_, orr,
):
    t = lax.axis_index("tok")
    r = lax.axis_index("row")
    c = lax.axis_index("col")
    k = lax.rem(t, 2)
    yh = lax.rem(lax.div(t, 2), 2)
    z = lax.div(t, 4)
    y = yh * 2 + r
    zp = lax.rem(z, 2)

    def dev(cx, cy, cz, ck):
        return ((cz * 2 + lax.div(cy, 2)) * 2 + ck, lax.rem(cy, 2), cx)

    def xo(i):
        return lax.rem(c + i, NX)

    def yo(i):
        return lax.rem(y + i, NY)

    def zo(i):
        return lax.rem(z + i, NZ)

    partner = dev(c, y, z, 1 - k)
    pending = []

    def send(src, dst, ssem, rsem, to):
        copy = pltpu.make_async_remote_copy(
            src_ref=src, dst_ref=dst, send_sem=ssem, recv_sem=rsem,
            device_id=to, device_id_type=MESH,
        )
        copy.start()
        pending.append(copy)

    def landed(dst, rsem):
        pltpu.make_async_copy(dst, dst, rsem).wait()

    own_x = pltpu.make_async_copy(x_ref, xall.at[c, k], lsem.at[0])
    own_g = pltpu.make_async_copy(g_ref, gall.at[c], lsem.at[1])
    def raw_rows(n):
        half = zp if n < 8 else 1 - zp
        off = (n % 2) * 512 + (n % 8) // 2 * 128
        return pl.ds(pl.multiple_of(half * 1024 + off, 128), 128)

    raw_copies = [
        pltpu.make_async_copy(w_ref.at[raw_rows(n)], raw.at[raw_rows(n)], lsem.at[2 + n])
        for n in range(16)
    ]
    for copy in raw_copies:
        copy.start()
    own_x.start()
    own_g.start()

    def unpack_w(n):
        raw_copies[n].wait()
        rows = raw_rows(n)
        heads = jnp.swapaxes(raw[rows], 0, 1)
        for hh in range(2):
            head = jnp.where(k == 0, heads[hh], heads[2 + hh])
            wqo[rows, hh * 128 : (hh + 1) * 128] = head[:, 0:128]
            wkvo[hh, rows, :] = head[:, 128:384]


    lane = lax.broadcasted_iota(jnp.int32, (1, 128), 1)
    ids = doc_ref[...]
    below = [jnp.sum((ids < d).astype(F32), axis=1, keepdims=True) for d in (1, 2, 3)]
    low = sum(jnp.where(lane == d + 1, below[d], 0.0) for d in range(3))
    high = sum(jnp.where(lane == d, below[d], 0.0) for d in range(3))
    sub = lax.broadcasted_iota(jnp.int32, (8, 128), 0)
    counts = jnp.where(sub == 0, low, jnp.where(sub == 1, high, 0.0))
    cnt[...] = counts
    cntall[0] = counts

    barrier = pltpu.get_barrier_semaphore()
    peers = [dev(xo(i), y, z, k) for i in (1, 2, 3)]
    peers += [dev(c, y, zo(1), k), dev(c, y, zo(NZ - 1), k)]
    plane = [(dy, dk) for dy in range(NY) for dk in range(2) if (dy, dk) != (0, 0)]
    core = (k, 1 - k)
    peers += [dev(c, yo(dy), z, core[dk]) for dy, dk in plane]
    for peer in peers:
        pl.semaphore_signal(barrier, inc=1, device_id=peer, device_id_type=MESH)
    unpack_w(0)
    unpack_w(1)
    pl.semaphore_wait(barrier, len(peers))

    yup, ydown = dev(c, yo(1), z, k), dev(c, yo(3), z, k)
    zup, zdown = dev(c, y, zo(1), k), dev(c, y, zo(NZ - 1), k)
    xup, xdown = dev(xo(1), y, z, k), dev(xo(3), y, z, k)
    for i in (1, 2, 3):
        send(g_ref, gall.at[c], gs.at[i - 1], gr.at[NX - i - 1], dev(xo(i), y, z, k))
    for n, (dy, dk) in enumerate(plane):
        rel = ((NY - dy) % NY) * 2 + dk
        send(cnt, cntall.at[rel], cs.at[n], cr.at[rel - 1], dev(c, yo(dy), z, core[dk]))
    cuts = (pl.ds(0, 48), pl.ds(48, 48), pl.ds(96, 48), pl.ds(144, 32))

    def send_wkv(s):
        for way, to in ((0, yup), (1, ydown)):
            off = way * 512 + s * PIECE
            send(
                wkvo.at[pl.ds(0, 2), pl.ds(pl.multiple_of(zp * 1024 + off, PIECE), PIECE), :],
                wkvx.at[zp, pl.ds(0, 2), pl.ds(off, PIECE), :],
                wys.at[way * SUBS + s], wyr.at[way * SUBS + s], to,
            )

    def send_x(i):
        send(x_ref.at[cuts[i], :], xall.at[c, k, cuts[i], :], xs.at[i], xr.at[i], xup)
        i = 3 - i
        send(x_ref.at[cuts[i], :], xall.at[c, k, cuts[i], :], xs.at[4 + i], xr.at[4 + i], xdown)

    left, right, far = xo(3), xo(1), xo(2)

    def relay_x(i):
        part = xall.at[left, k, cuts[i], :]
        landed(part, xr.at[i])
        send(part, part, xs.at[8 + i], xr.at[8 + i], xup)
        i = 3 - i
        part = xall.at[right, k, cuts[i], :]
        landed(part, xr.at[4 + i])
        send(part, part, xs.at[8 + i], xr.at[8 + i], xdown)

    send_wkv(0)
    send_x(0)
    send_wkv(1)
    unpack_w(2)
    unpack_w(3)
    send_x(1)
    unpack_w(4)
    unpack_w(5)
    send_wkv(2)
    send_wkv(3)

    def send_wq(s):
        for way, to in ((0, yup), (1, ydown)):
            rows = pl.ds(way * 1024 + s * QPIECE, QPIECE)
            n = way * QSUBS + s
            send(wqo.at[rows, :], wqx.at[rows, :], wqs.at[n], wqr.at[n], to)

    for n in range(6, 16):
        unpack_w(n)

    row = lax.broadcasted_iota(jnp.int32, (2 * ROWS, 128), 0)
    lanes = lax.broadcasted_iota(jnp.int32, (2 * ROWS, 128), 1)
    place = (z * 8 + yh * 4 + r) * ROWS + row + jnp.where(row >= ROWS, ROWS, 0)
    angle = place.astype(F32) * inv_ref[...]
    cosb[...] = jnp.cos(angle)
    sine = jnp.sin(angle)
    sinb[...] = jnp.where(lanes < 64, -sine, sine)

    for n in range(7):
        landed(cntall.at[n + 1], cr.at[n])
    total = cntall[0]
    for n in range(7):
        total = total + cntall[n + 1]
    lane8 = lax.broadcasted_iota(jnp.int32, (8, 128), 1)
    bnd[z] = jnp.where((sub == 1) & (lane8 >= 3), BIG, total)

    def forward_w(s):
        for way, to in ((0, zup), (1, zdown)):
            rows = pl.ds(way * 512 + s * PIECE, PIECE)
            piece = wkvx.at[zp, pl.ds(0, 2), rows, :]
            landed(piece, wyr.at[way * SUBS + s])
            send(piece, piece, wzs.at[way * SUBS + s], wzr.at[way * SUBS + s], to)

    def bounds_hop(d):
        if d > 0:
            landed(bnd.at[zo(NZ - d)], br.at[2 * (d - 1)])
            if d < 4:
                landed(bnd.at[zo(d)], br.at[2 * (d - 1) + 1])
        if d < 4:
            send(bnd.at[zo(NZ - d)], bnd.at[zo(NZ - d)], bs.at[2 * d], br.at[2 * d], zup)
        if d < 3:
            send(bnd.at[zo(d)], bnd.at[zo(d)], bs.at[2 * d + 1], br.at[2 * d + 1], zdown)

    send_x(2)
    forward_w(0)
    send_wkv(4)
    forward_w(1)
    send_wkv(5)
    send_x(3)
    bounds_hop(0)
    relay_x(0)
    relay_x(1)
    send(x_ref, xall.at[c, k], ps.at[0], pr.at[0], partner)
    forward_w(2)
    send_wkv(6)
    forward_w(3)
    send_wkv(7)
    bounds_hop(1)
    for i in (2, 3):
        landed(xall.at[left, k, cuts[i], :], xr.at[i])
        landed(xall.at[right, k, cuts[3 - i], :], xr.at[7 - i])
    send(xall.at[left, k], xall.at[left, k], ps.at[1], pr.at[1], partner)
    send(xall.at[right, k], xall.at[right, k], ps.at[2], pr.at[2], partner)
    forward_w(4)
    send_wq(0)
    forward_w(5)
    bounds_hop(2)
    for i in range(4):
        landed(xall.at[far, k, cuts[i], :], xr.at[8 + i])
    send(xall.at[far, k], xall.at[far, k], ps.at[3], pr.at[3], partner)
    forward_w(6)
    forward_w(7)
    send_wq(1)
    own_x.wait()
    own_g.wait()
    for i in (1, 2, 3):
        landed(gall.at[xo(i)], gr.at[i - 1])

    def normalise(kk, at):
        squares = jnp.zeros((ROWS, 128), F32)
        for cc in range(NX):
            for s in range(8):
                v = xall[cc, kk, :, s * 128 : (s + 1) * 128].astype(F32)
                squares = squares + v * v
        mean = jnp.sum(squares, axis=1, keepdims=True) * (1.0 / (NX * WIDTH))
        inverse = jnp.broadcast_to(lax.rsqrt(mean + 1e-05), (ROWS, 128))
        for cc in range(NX):
            for s in range(8):
                v = xall[cc, kk, :, s * 128 : (s + 1) * 128].astype(F32)
                gain = gall[cc, s : s + 1, :].astype(F32)
                xn[cc, at, s * 128 : (s + 1) * 128] = (v * inverse * gain).astype(BF16)

    normalise(k, pl.ds(pl.multiple_of(k * ROWS, ROWS), ROWS))
    for n, block in enumerate((c, left, right, far)):
        landed(xall.at[block, 1 - k], pr.at[n])
    normalise(1 - k, pl.ds(pl.multiple_of((1 - k) * ROWS, ROWS), ROWS))
    for hh in range(2):
        out = slice(hh * 256, (hh + 1) * 256)
        acc[:, out] = jnp.dot(xn[2 * r], wkvo[hh, 0:1024], preferred_element_type=F32)
        acc[:, out] += jnp.dot(xn[2 * r + 1], wkvo[hh, 1024:2048], preferred_element_type=F32)
    for hh in range(2):
        out = slice(hh * 256, (hh + 1) * 256)
        acc[:, out] += jnp.dot(xn[2 * (1 - r) + zp], wkvx[zp, hh], preferred_element_type=F32)
    for s in range(SUBS):
        for way in range(2):
            landed(
                wkvx.at[1 - zp, pl.ds(0, 2), pl.ds(way * 512 + s * PIECE, PIECE), :],
                wzr.at[way * SUBS + s],
            )
    for hh in range(2):
        out = slice(hh * 256, (hh + 1) * 256)
        acc[:, out] += jnp.dot(xn[2 * (1 - r) + 1 - zp], wkvx[1 - zp, hh], preferred_element_type=F32)

    def kv_at(p, zz, yy):
        return kv.at[p, zz, lax.div(yy, 2), pl.ds(0, 2), lax.rem(yy, 2)]

    for hh in range(2):
        u = acc[:, hh * 256 : hh * 256 + 128]
        u = u * cosb[...] + pltpu.roll(u, 64, 1) * sinb[...]
        stg[hh, 0, 0] = u[:ROWS].astype(BF16)
        stg[hh, 0, 1] = u[ROWS:].astype(BF16)
        u = acc[:, hh * 256 + 128 : hh * 256 + 256]
        stg[hh, 1, 0] = u[:ROWS].astype(BF16)
        stg[hh, 1, 1] = u[ROWS:].astype(BF16)
    exchange = []

    def exchange_send(source, slot_of, ssems, rsems):
        for step in range(2):
            hh = step
            yd = 2 * k + hh
            rel = lax.rem(y - yd + NY, NY)
            for j in range(2):
                here = jnp.logical_and(yd == y, k == j)
                to = dev(c, yd, z, j)
                move = (source.at[hh, j], slot_of(j), ssems.at[hh * 2 + j], rsems.at[rel])

                @pl.when(here)
                def _():
                    pltpu.make_async_copy(move[0], move[1], move[3]).start()

                @pl.when(jnp.logical_not(here))
                def _():
                    pltpu.make_async_remote_copy(
                        src_ref=move[0], dst_ref=move[1], send_sem=move[2], recv_sem=move[3],
                        device_id=to, device_id_type=MESH,
                    ).start()

                exchange.append((here, move, to))

    exchange_send(stg, lambda j: kv_at(j, z, y), as_, akr)
    send_wq(2)
    send_wq(3)

    def ring_start(u):
        block = kv_at(k, z, yo(u))
        landed(block, akr.at[u])
        send(block, block, rs.at[u], rp.at[u], zup)
        send(block, block, rs.at[4 + u], rm.at[u], zdown)
        send(block, block, pks.at[u], pkr.at[u], partner)

    ring_start(0)
    accq[...] = jnp.dot(xn[2 * r], wqo[0:1024, :], preferred_element_type=F32)
    accq[...] += jnp.dot(xn[2 * r + 1], wqo[1024:2048, :], preferred_element_type=F32)

    def project_q(part):
        for s in (2 * part, 2 * part + 1):
            for way in range(2):
                landed(
                    wqx.at[pl.ds(way * 1024 + s * QPIECE, QPIECE), :], wqr.at[way * QSUBS + s]
                )
        low = part * 512
        for way in range(2):
            accq[...] += jnp.dot(
                xn[2 * (1 - r) + way, :, low : low + 512],
                wqx[way * 1024 + low : way * 1024 + low + 512, :],
                preferred_element_type=F32,
            )


    def ring(d, pieces):
        up, down = zo(NZ - d), zo(d)
        for u in pieces:
            if d < 4 or u in PLUS:
                block = kv_at(k, up, yo(u))
                landed(block, rp.at[(d - 1) * 4 + u])
                if d < 3 or (d == 3 and u in PLUS):
                    send(block, block, rs.at[d * 8 + u], rp.at[d * 4 + u], zup)
                n = (2 * d - 1) * 4 + u
                send(block, block, pks.at[n], pkr.at[n], partner)
            if d < 4 or u in MINUS:
                block = kv_at(k, down, yo(u))
                landed(block, rm.at[(d - 1) * 4 + u])
                if d < 3 or (d == 3 and u in MINUS):
                    send(block, block, rs.at[d * 8 + 4 + u], rm.at[d * 4 + u], zdown)
                n = (2 * d if d < 4 else 7) * 4 + u
                send(block, block, pks.at[n], pkr.at[n], partner)
    ring(1, (0,))
    ring_start(1)
    ring_start(3)
    ring_start(2)
    bounds_hop(3)
    project_q(0)
    ring(2, (0,))
    project_q(1)
    for hh in range(2):
        u = accq[:, hh * 128 : (hh + 1) * 128]
        u = u * cosb[...] + pltpu.roll(u, 64, 1) * sinb[...]
        stgq[hh, 0] = u[:ROWS].astype(BF16)
        stgq[hh, 1] = u[ROWS:].astype(BF16)
    exchange_send(stgq, lambda j: qb.at[y], aqs, aqr)

    ring(1, (1, 3, 2))
    bounds_hop(4)

    mrun[...] = jnp.full_like(mrun, HIDE)
    oacc[...] = jnp.zeros_like(oacc)
    qrow = lax.broadcasted_iota(jnp.int32, (4 * ROWS, 128), 0)
    qplace = (qrow + jnp.where(qrow >= 2 * ROWS, 2 * ROWS, 0) + 2 * ROWS * k).astype(F32)
    mine = bnd[z]
    inside = (qplace >= mine[0:1, :]) & (qplace < mine[1:2, :])
    qcat[:, 128:256] = jnp.where(inside, 1.0, 0.0).astype(BF16)
    for u in ORDER:
        landed(qb.at[yo(u)], aqr.at[u])
    for n in range(4):
        qcat[n * ROWS : (n + 1) * ROWS, 0:128] = qb[n]

    def out_copy(yq):
        return pltpu.make_async_remote_copy(
            src_ref=osend.at[yq], dst_ref=obuf.at[y], send_sem=os_.at[yq],
            recv_sem=orr.at[lax.rem(y - yq + NY, NY)],
            device_id=dev(c, yq, z, k), device_id_type=MESH,
        )

    def tile_rows(i):
        if isinstance(i, int):
            return slice(i * 2 * ROWS, (i + 1) * 2 * ROWS)
        return pl.ds(pl.multiple_of(i * (2 * ROWS), 2 * ROWS), 2 * ROWS)

    near = 1 - lax.rem(y, 2)

    def out_tile(i):
        rows = tile_rows(i)
        result = (oacc[rows, 0:128] / oacc[rows, 128:256]).astype(BF16)
        for n in range(2):
            osend[2 * i + n] = result[n * ROWS : (n + 1) * ROWS]
        for n in (near, 1 - near):
            yq = 2 * i + n

            @pl.when(y == yq)
            def _():
                obuf[yq] = osend[yq]

            @pl.when(y != yq)
            def _():
                out_copy(yq).start()

    def attend(zz, diagonal, tiles=(0, 1), after=None):
        limit = bnd[zz]
        krow = lax.broadcasted_iota(jnp.int32, (8 * ROWS, 128), 0).astype(F32)
        kin = (krow >= limit[0:1, :]) & (krow < limit[1:2, :])
        kaug[...] = jnp.where(kin, 0.0, HIDE).astype(BF16)

        keys = jnp.concatenate([kv[0, zz].reshape(8 * ROWS, 128), kaug[...]], axis=1)
        values = kv[1, zz].reshape(8 * ROWS, 128)
        values = jnp.concatenate([values, jnp.ones_like(values)], axis=1)

        def scored(i):
            rows = tile_rows(i)
            return lax.dot_general(
                qcat[rows, :], keys, (((1,), (1,)), ((), ())), preferred_element_type=F32
            )

        def absorb(i, scores):
            rows = tile_rows(i)
            if diagonal:
                shape = (2 * ROWS, 8 * ROWS)
                qp = lax.broadcasted_iota(jnp.int32, shape, 0) + i * 4 * ROWS + 2 * ROWS * k
                kp = lax.broadcasted_iota(jnp.int32, shape, 1)
                scores = jnp.where(kp <= qp, scores, HIDE)
            before = mrun[rows, :]
            newest = jnp.maximum(before, jnp.max(scores, axis=1, keepdims=True))
            weights = jnp.exp2((scores - newest[:, 0:1]) * SCALE).astype(BF16)
            factor = jnp.exp2((before - newest) * SCALE)
            added = jnp.dot(weights, values, preferred_element_type=F32)
            oacc[rows, :] = oacc[rows, :] * jnp.concatenate([factor, factor], axis=1) + added
            mrun[rows, :] = newest

        first = scored(tiles[0])
        second = scored(tiles[1])
        for i, scores in zip(tiles, (first, second)):
            absorb(i, scores)
            if after is not None:
                after(i)

    def shared(zz, n):
        for u in ORDER:
            landed(kv_at(1 - k, zz, yo(u)), pkr.at[n * 4 + u])

    def attend_up(d):
        shared(zo(NZ - d), 2 * d - 1)

        @pl.when(z >= d)
        def _():
            attend(zo(NZ - d), False)

    def attend_down(d):
        shared(zo(d), 2 * d)

        @pl.when(z + d >= NZ)
        def _():
            attend(zo(d), False)

    shared(z, 0)
    attend(z, True)
    ring(3, (0,))
    ring(2, (1,))
    attend_up(1)
    ring(2, (3, 2))
    attend_down(1)
    attend_up(2)
    ring(4, (0,))
    ring(3, (1,))
    attend_down(2)
    ring(3, (3, 2))
    attend_up(3)
    ring(4, (3,))
    attend_down(3)
    ring(4, (1, 2))
    shared(zo(4), 7)

    @pl.when(z >= 4)
    def _():
        attend(zo(4), False, (1 - yh, yh), out_tile)

    @pl.when(z < 4)
    def _():
        out_tile(1 - yh)
        out_tile(yh)

    for dy in (1, 2, 3):
        landed(obuf.at[yo(dy)], orr.at[dy])
    for h in range(4):
        o_ref[:, h * 128 : (h + 1) * 128] = obuf[h]

    for here, move, to in exchange:

        @pl.when(jnp.logical_not(here))
        def _():
            pltpu.make_async_remote_copy(
                src_ref=move[0], dst_ref=move[1], send_sem=move[2], recv_sem=move[3],
                device_id=to, device_id_type=MESH,
            ).wait_send()

    for yq in range(NY):

        @pl.when(y != yq)
        def _():
            out_copy(yq).wait_send()

    for copy in pending:
        copy.wait_send()


def per_device(activations, norm_gain, qkv_weight, doc_ids):
    spacing = np.arange(64).astype(np.float32) * np.float32(2.0 / 128)
    inverse = np.power(np.float32(10000.0), -spacing).astype(np.float32)
    inverse = np.concatenate([inverse, inverse])[None, :]
    dma = pltpu.SemaphoreType.DMA
    anywhere = pl.BlockSpec(memory_space=pl.ANY)
    local = pl.BlockSpec(memory_space=pltpu.VMEM)
    scratch = [
        pltpu.VMEM((NX, 2, ROWS, WIDTH), BF16),
        pltpu.VMEM((NX, 8, 128), BF16),
        pltpu.VMEM((HALF, 4, 384), BF16),
        pltpu.VMEM((2, HALF, 256), BF16),
        pltpu.VMEM((2, 2, 1024, 256), BF16),
        pltpu.VMEM((HALF, 256), BF16),
        pltpu.VMEM((HALF, 256), BF16),
        pltpu.VMEM((8, 128), F32),
        pltpu.VMEM((8, 8, 128), F32),
        pltpu.VMEM((NZ, 8, 128), F32),
        pltpu.VMEM((NX, 2 * ROWS, WIDTH), BF16),
        pltpu.VMEM((2 * ROWS, 512), F32),
        pltpu.VMEM((2 * ROWS, 256), F32),
        pltpu.VMEM((2 * ROWS, 128), F32),
        pltpu.VMEM((2 * ROWS, 128), F32),
        pltpu.VMEM((2, 2, 2, ROWS, 128), BF16),
        pltpu.VMEM((2, 2, ROWS, 128), BF16),
        pltpu.VMEM((2, NZ, 2, 2, 2, ROWS, 128), BF16),
        pltpu.VMEM((NY, ROWS, 128), BF16),
        pltpu.VMEM((4 * ROWS, 256), BF16),
        pltpu.VMEM((8 * ROWS, 128), BF16),
        pltpu.VMEM((4 * ROWS, 128), F32),
        pltpu.VMEM((4 * ROWS, 256), F32),
        pltpu.VMEM((NY, ROWS, 128), BF16),
        pltpu.VMEM((NY, ROWS, 128), BF16),
        dma((18,)),
        dma((2 * SUBS,)), dma((2 * SUBS,)),
        dma((2 * SUBS,)), dma((2 * SUBS,)),
        dma((2 * QSUBS,)), dma((2 * QSUBS,)),
        dma((12,)), dma((12,)),
        dma((3,)), dma((3,)),
        dma((4,)), dma((4,)),
        dma((7,)), dma((7,)),
        dma((8,)), dma((8,)),
        dma((4,)), dma((4,)), dma((4,)), dma((4,)),
        dma((32,)), dma((16,)), dma((16,)),
        dma((32,)), dma((32,)),
        dma((4,)), dma((4,)),
    ]
    return pl.pallas_call(
        kernel,
        out_shape=jax.ShapeDtypeStruct((ROWS, 512), BF16),
        in_specs=[anywhere, anywhere, anywhere, local, local],
        out_specs=local,
        scratch_shapes=scratch,
        compiler_params=pltpu.CompilerParams(
            collective_id=0, has_side_effects=True, vmem_limit_bytes=60 * 1024 * 1024
        ),
        name="attention_block",
    )(
        activations, norm_gain.reshape(8, 128), qkv_weight, doc_ids.reshape(1, ROWS), jnp.asarray(inverse)
    )


def solution(mesh):
    placed = (P(("tok", "row"), "col"), P("col"), P("row", "col", None), P(("tok", "row")))
    return jax.shard_map(
        per_device, mesh=mesh, in_specs=placed, out_specs=P(("tok", "row"), "col"), check_vma=False
    )
```
